32 devices in a mesh: slab: 2 (over x), cell: 8 (over z, y), dp: 2 (over core).
Axes of the slice: x: 2, y: 2, z: 4, core: 2. Of those that a mesh axis runs over, the one named last changes fastest.
Arguments:
- sens: float32 [2, 2048, 32768], P(None, ('slab', 'dp'), 'cell'), parts along dimension 1, may hold values from -0.03125 to 0.03125
- observed: float32 [2, 2048], P(None, ('slab', 'dp')), parts along dimension 1, may hold values from -6 to 6
- noise: float32 [2, 2048], P(None, ('slab', 'dp')), parts along dimension 1, may hold values from 0.5 to 2
- survey_ids: int32 [2, 2048], P(None, ('slab', 'dp')), parts along dimension 1, may hold values from 0 to 7
- data_perturb: float32 [2, 8, 2048], P(None, None, ('slab', 'dp')), parts along dimension 2, may hold values from -6 to 6
- prior: float32 [2, 16, 32, 1024], P(None, 'slab', 'cell'), parts along dimension 1, may hold values from -6 to 6
Outputs:
- models: float32 [2, 16, 32, 1024], P(None, 'slab', 'cell'), parts along dimension 1
The draws below stay inside these ranges and needn't reach their ends.
There are 2 independent parts, one for each index of `slab`. The reference program is written for one: setup_inputs(seed, part) draws one part's arguments, and reference() takes and returns one part's arrays. A program takes and returns all parts, laid end to end along the dimension named above; each array names one. Nothing has to cross between parts.
All inputs are finite; a program needn't handle non-finite values.
Results may differ from the reference program's by a relative error of at most 0.0001.
Values sent between devices are 32-bit elements; how exact they have to be, the bound alone decides.
A program may use at most 64 MiB of HBM per device.

```python
import math
import jax
import jax.numpy as jnp
from jax import lax

NX = 32
NY = 32
NZ = 32
MODELS = 8
NSURV = 8
ITERS = 4
ND = 1024
NC = 32768


def set_ends(values, key, smallest, high):
    shape = values.shape
    spot = [jax.random.randint(jax.random.fold_in(key, axis), (), 0, shape[axis]) for axis in range(len(shape))]
    values = values.at[tuple(spot)].set(smallest)
    longest = shape.index(max(shape))
    spot[longest] = (spot[longest] + 1) % shape[longest]
    return values.at[tuple(spot)].set(high)


def shard_levels(rng, shape, shards, least, largest):
    def one(dim, blocks):
        steps = jax.random.uniform(jax.random.fold_in(jax.random.fold_in(rng, 6), dim), (blocks,), jnp.float32, least / len(shards), largest / len(shards))
        return jnp.repeat(jnp.exp(steps), shape[dim] // blocks).reshape((-1,) + (1,) * (len(shape) - dim - 1))

    loudness = one(*shards[0])
    for cut in shards[1:]:
        loudness = loudness * one(*cut)
    return loudness


def normal_values(stream_key, shape, scale, most, split=(), kind=jnp.bfloat16):
    result = scale * jax.random.normal(stream_key, shape, jnp.float32)
    if split:
        result = result * shard_levels(stream_key, shape, split, -0.22, 0.18)
    return jnp.clip(result, -most, most).astype(kind)


def setup_inputs(seed: int = 0, part: int = 0) -> dict:
    splits = jax.random.split(jax.random.key(seed), 7)
    part_keys = jax.random.split(jax.random.fold_in(splits[6], part), 7)
    return {
        "sens": normal_values(part_keys[0], (2, ND, NC), NC ** -0.5, 0.03125, ((1, 2), (2, 8)), jnp.float32),
        "observed": normal_values(part_keys[1], (2, ND), 1.0, 6.0, ((1, 2),), jnp.float32),
        "noise": jnp.clip(jnp.exp(math.log(2.0) - 1.3862944 * jax.random.uniform(part_keys[2], (2, ND), jnp.float32) ** shard_levels(part_keys[2], (2, ND), ((1, 2),), -0.2, 0.2)), 0.5, 2.0),
        "survey_ids": set_ends(jax.random.randint(part_keys[3], (2, ND), 0, NSURV), jax.random.fold_in(part_keys[3], 1), 0, NSURV - 1).astype(jnp.int32),
        "data_perturb": normal_values(part_keys[4], (2, MODELS, ND), 1.0, 6.0, ((2, 2),), jnp.float32),
        "prior": normal_values(part_keys[5], (2, MODELS, NZ, NY * NX), 1.0, 6.0, ((2, 8),), jnp.float32),
    }


nu_value = 4.0
step_size = 0.5
couple_weight = 0.02
prior_weight = 0.1

def forward_diff(field, axis):
    length = field.shape[axis]
    following = jnp.concatenate([lax.slice_in_dim(field, 1, length, axis=axis), jnp.zeros_like(lax.slice_in_dim(field, 0, 1, axis=axis))], axis=axis)
    keep_shape = [1] * field.ndim
    keep_shape[axis] = length
    keeper = (jnp.arange(length) < length - 1).astype(jnp.float32).reshape(keep_shape)
    return ((following - field) * keeper, keeper)

def backward_diff(values, keeper, axis):
    length = values.shape[axis]
    masked = values * keeper
    preceding = jnp.concatenate([jnp.zeros_like(lax.slice_in_dim(masked, 0, 1, axis=axis)), lax.slice_in_dim(masked, 0, length - 1, axis=axis)], axis=axis)
    return preceding - masked

def coupling(fields):
    diffs = []
    keepers = []
    for axis in (4, 3, 2):
        change, keeper = forward_diff(fields, axis)
        diffs.append(change)
        keepers.append(keeper)
    first = [change[0] for change in diffs]
    second = [change[1] for change in diffs]
    cross_x = first[1] * second[2] - first[2] * second[1]
    cross_y = first[2] * second[0] - first[0] * second[2]
    cross_z = first[0] * second[1] - first[1] * second[0]
    scaling = 2.0 / (1.0 + cross_x * cross_x + cross_y * cross_y + cross_z * cross_z)
    grad_first = [scaling * (second[1] * cross_z - second[2] * cross_y), scaling * (second[2] * cross_x - second[0] * cross_z), scaling * (second[0] * cross_y - second[1] * cross_x)]
    grad_second = [scaling * (cross_y * first[2] - cross_z * first[1]), scaling * (cross_z * first[0] - cross_x * first[2]), scaling * (cross_x * first[1] - cross_y * first[0])]
    total = jnp.zeros_like(fields)
    for index, axis in enumerate((4, 3, 2)):
        stacked = jnp.stack([grad_first[index], grad_second[index]])
        total = total + backward_diff(stacked, keepers[index], axis)
    return total

def reference(sens, observed, noise, survey_ids, data_perturb, prior):
    highest = lax.Precision.HIGHEST
    targets = observed[:, None, :] + noise[:, None, :] * data_perturb
    labels = jnp.arange(NSURV, dtype=jnp.int32)
    one_hot = (survey_ids[:, :, None] == labels).astype(jnp.float32)
    counts = lax.optimization_barrier(jnp.sum(one_hot, axis=1))
    models = prior
    for iteration in range(ITERS):
        flattened = models.reshape(2, MODELS, NZ * NY * NX)
        predicted = jnp.einsum('skc,snc->skn', flattened, sens, precision=highest)
        resid = (predicted - targets) / noise[:, None, :]
        sums = jnp.einsum('skn,snj->skj', resid * resid, one_hot, precision=highest)
        spread = (sums + 1.0) / (counts[:, None, :] + 1.0)
        spread_rows = jnp.einsum('skj,snj->skn', spread, one_hot, precision=highest)
        scale_rows = jnp.sqrt(spread_rows)
        whitened = resid / scale_rows
        factor = (nu_value + 1.0) / (nu_value + whitened * whitened) * whitened / (noise[:, None, :] * scale_rows)
        gradient = jnp.einsum('skn,snc->skc', factor, sens, precision=highest).reshape(2, MODELS, NZ, NY * NX)
        grid_field = models.reshape(2, MODELS, NZ, NY, NX)
        couple = coupling(grid_field).reshape(2, MODELS, NZ, NY * NX)
        models = models - step_size * (gradient + couple_weight * couple + prior_weight * (models - prior))
    return models
```

```python
import functools

import jax
import jax.numpy as jnp
from jax import lax
from jax.experimental import pallas as pl
from jax.experimental.pallas import tpu as pltpu
from jax.sharding import PartitionSpec as P

NX = 32
NZ = 32
NSURV = 8
ITERS = 4
LANES = 128

nu_value = 4.0
step_size = 0.5
couple_weight = 0.02
prior_weight = 0.1

MESH = pl.DeviceIdType.MESH


def split_rows(value):
    high = value.astype(jnp.bfloat16).astype(jnp.float32)
    return jnp.concatenate([high, value - high], axis=0).astype(jnp.bfloat16)


def fold_rows(value):
    half = value.shape[0] // 2
    return value[:half] + value[half:]


def cross_gradients(first, second, masks, layer_cells, z_on):
    along_x, along_y = masks

    def differences(field, deeper):
        diff_x = (pltpu.roll(field, layer_cells - 1, 1) - field) * along_x
        diff_y = (pltpu.roll(field, layer_cells - NX, 1) - field) * along_y
        return diff_x, diff_y, (deeper - field) * z_on

    a = differences(*first)
    b = differences(*second)
    tx = a[1] * b[2] - a[2] * b[1]
    ty = a[2] * b[0] - a[0] * b[2]
    tz = a[0] * b[1] - a[1] * b[0]
    scaling = 2.0 / (1.0 + tx * tx + ty * ty + tz * tz)
    sx = scaling * along_x
    sy = scaling * along_y
    sz = scaling * z_on
    return (
        (sx * (b[1] * tz - b[2] * ty), sy * (b[2] * tx - b[0] * tz), sz * (b[0] * ty - b[1] * tx)),
        (sx * (ty * a[2] - tz * a[1]), sy * (tz * a[0] - tx * a[2]), sz * (tx * a[1] - ty * a[0])),
    )


def kernel(
    cells, sens, observed, noise, survey_ids, perturb, prior, out,
    raw, high, low, high_t, low_t, base, carry_z, halo_up, halo_dn, acc, gather, target, per_noise, resids,
    count_tile, sums_mine, sums_other, rows, grad_mine, grad_other,
    load_sem, halo_send, halo_recv, part_send, part_recv, sums_send, sums_recv, grad_send, grad_recv,
):
    stations = observed.shape[1]
    layers, layer_cells = prior.shape[1], prior.shape[3]
    tiles = stations // LANES
    slab = lax.axis_index("slab")
    me = lax.axis_index("cell")
    dp = lax.axis_index("dp")
    partner = 1 - dp

    def load(s, l):
        return pltpu.make_async_copy(
            sens.at[s, :, pl.ds(pl.multiple_of(l * layer_cells, LANES), layer_cells)], raw.at[s, l],
            load_sem.at[s, l],
        )

    for s in range(2):
        for l in range(layers):
            load(s, l).start()

    barrier = pltpu.get_barrier_semaphore()
    pl.semaphore_signal(barrier, inc=1, device_id=(slab, me, partner), device_id_type=MESH)
    for k in range(1, cells):
        there = lax.rem(me + k, cells)
        pl.semaphore_signal(barrier, inc=1, device_id=(slab, there, dp), device_id_type=MESH)

    position = lax.broadcasted_iota(jnp.int32, (1, layer_cells), 1)
    masks = (
        (lax.rem(position, NX) < NX - 1).astype(jnp.float32),
        (position < layer_cells - NX).astype(jnp.float32),
    )
    lane = lax.broadcasted_iota(jnp.int32, (8, LANES), 1)

    @pl.when(me == cells - 1)
    def _():
        halo_up[...] = jnp.zeros_like(halo_up)

    @pl.when(me == 0)
    def _():
        halo_dn[...] = jnp.zeros_like(halo_dn)

    def ids_at(s, t):
        return jnp.broadcast_to(survey_ids[s : s + 1, t * LANES : (t + 1) * LANES], (8, LANES))

    def by_survey(s, values, offset):
        total = jnp.zeros((8, LANES), jnp.float32)
        ids = [ids_at(s, t) for t in range(tiles)]
        for j in range(NSURV):
            one = jnp.where(ids[0] == j, values[0], 0.0)
            for t in range(1, tiles):
                one = one + jnp.where(ids[t] == j, values[t], 0.0)
            total = jnp.where(lane == j + offset, jnp.sum(one, axis=1, keepdims=True), total)
        return total

    for s in range(2):
        count_tile[s] = by_survey(s, [jnp.ones((8, LANES), jnp.float32)] * tiles, NSURV)
        scale = noise[s : s + 1]
        target[s] = observed[s : s + 1] + scale * perturb[s]
        per_noise[s] = jnp.broadcast_to(1.0 / scale, per_noise.shape[1:])

    def halo_copy(source, it, s, up):
        return pltpu.make_async_remote_copy(
            src_ref=source.at[s, 0 if up else layers - 1],
            dst_ref=(halo_up if up else halo_dn).at[it, s],
            send_sem=halo_send.at[s, 0 if up else 1],
            recv_sem=halo_recv.at[it, s, 0 if up else 1],
            device_id=(slab, jnp.maximum(me - 1, 0) if up else jnp.minimum(me + 1, cells - 1), dp),
            device_id_type=MESH,
        )

    def start_halo(source, it, s, l):
        if l == 0:
            @pl.when(me > 0)
            def _():
                halo_copy(source, it, s, True).start()

        if l == layers - 1:
            @pl.when(me < cells - 1)
            def _():
                halo_copy(source, it, s, False).start()

    def wait_halo_sent(source, it, s):
        @pl.when(me > 0)
        def _():
            halo_copy(source, it, s, True).wait_send()

        @pl.when(me < cells - 1)
        def _():
            halo_copy(source, it, s, False).wait_send()

    def wait_halo_here(source, it, s):
        @pl.when(me < cells - 1)
        def _():
            halo_copy(source, it, s, True).wait_recv()

        @pl.when(me > 0)
        def _():
            halo_copy(source, it, s, False).wait_recv()

    def send_parts(it, s):
        gather[it, s, me] = fold_rows(acc[...])
        for k in range(1, cells):
            pltpu.make_async_remote_copy(
                src_ref=gather.at[it, s, me], dst_ref=gather.at[it, s, me],
                send_sem=part_send.at[s], recv_sem=part_recv.at[it, s],
                device_id=(slab, lax.rem(me + k, cells), dp), device_id_type=MESH,
            ).start()

    def wait_parts_sent(it, s):
        sent = gather.at[it, s, pl.ds(0, cells - 1)]
        pltpu.make_async_copy(sent, sent, part_send.at[s]).wait()

    def sums_copy(it, s):
        return pltpu.make_async_remote_copy(
            src_ref=sums_mine.at[it, s], dst_ref=sums_other.at[it, s],
            send_sem=sums_send.at[s], recv_sem=sums_recv.at[it, s],
            device_id=(slab, me, partner), device_id_type=MESH,
        )

    def residuals(it, s):
        got = gather.at[it, s, pl.ds(0, cells - 1)]
        pltpu.make_async_copy(got, got, part_recv.at[it, s]).wait()
        squares = []
        for t in range(tiles):
            span = slice(t * LANES, (t + 1) * LANES)
            predicted = gather[it, s, 0, :, span]
            for c in range(1, cells):
                predicted = predicted + gather[it, s, c, :, span]
            resid = (predicted - target[s, :, span]) * per_noise[s, :, span]
            resids[s, :, span] = resid
            squares.append(resid * resid)
        sums_mine[it, s] = by_survey(s, squares, 0) + count_tile[s]
        sums_copy(it, s).start()

    def weigh(it, s):
        sums_copy(it, s).wait_recv()
        sums = sums_mine[it, s] + sums_other[it, s]
        counts = pltpu.roll(sums, LANES - NSURV, 1)
        per_root = lax.rsqrt((sums + 1.0) / (counts + 1.0))
        columns = [jnp.broadcast_to(per_root[:, j : j + 1], (8, LANES)) for j in range(NSURV)]
        for t in range(tiles):
            span = slice(t * LANES, (t + 1) * LANES)
            ids = ids_at(s, t)
            per_scale = columns[0]
            for j in range(1, NSURV):
                per_scale = jnp.where(ids == j, columns[j], per_scale)
            whitened = resids[s, :, span] * per_scale
            factor = (
                (nu_value + 1.0) * whitened * (per_noise[s, :, span] * per_scale)
                / (nu_value + whitened * whitened)
            )
            rows[s, :, span] = split_rows(factor)

    def grad_copy(it, s, l):
        return pltpu.make_async_remote_copy(
            src_ref=grad_mine.at[s, l], dst_ref=grad_other.at[it, s, l],
            send_sem=grad_send.at[s, l], recv_sem=grad_recv.at[it, s, l],
            device_id=(slab, me, partner), device_id_type=MESH,
        )

    def gradient(it, s):
        for l in range(layers):
            factor = rows[s]
            product = jnp.dot(factor, high[s, l], preferred_element_type=jnp.float32)
            product = product + jnp.dot(factor, low[s, l], preferred_element_type=jnp.float32)
            grad_mine[s, l] = fold_rows(product)
            grad_copy(it, s, l).start()

    def predict(s, l, value):
        model = split_rows(value)
        product = jnp.dot(model, high_t[s, l], preferred_element_type=jnp.float32)
        product = product + jnp.dot(model, low_t[s, l], preferred_element_type=jnp.float32)
        acc[...] += product

    def couple(source, it):
        for l in range(layers):
            if l == 0:
                z_on = (me > 0).astype(jnp.float32)
                first, second = [(halo_dn[it, s], source[s, 0]) for s in range(2)]
                ga, gb = cross_gradients(first, second, masks, layer_cells, z_on)
                carry_z[0] = ga[2]
                carry_z[1] = gb[2]
            z_on = (me * layers + l < NZ - 1).astype(jnp.float32)
            first, second = [
                (source[s, l], source[s, l + 1] if l < layers - 1 else halo_up[it, s]) for s in range(2)
            ]
            both = cross_gradients(first, second, masks, layer_cells, z_on)
            for s in range(2):
                gx, gy, gz = both[s]
                total = pltpu.roll(gx, 1, 1) - gx + (pltpu.roll(gy, NX, 1) - gy) + (carry_z[s] - gz)
                carry_z[s] = gz
                field = source[s, l]
                base[s, l] = field - step_size * (
                    couple_weight * total + prior_weight * (field - prior[s, l])
                )

    def step(source, it, last):
        for s in range(2):
            residuals(it, s)
            if s == 0:
                for other in range(2):
                    wait_halo_here(source, it, other)
                couple(source, it)
            weigh(it, s)
            gradient(it, s)
            wait_halo_sent(source, it, s)
            acc[...] = jnp.zeros_like(acc)
            for l in range(layers):
                grad_copy(it, s, l).wait_recv()
                value = base[s, l] - step_size * (grad_mine[s, l] + grad_other[it, s, l])
                out[s, l] = value
                if not last:
                    start_halo(out, it + 1, s, l)
                    predict(s, l, value)
            wait_parts_sent(it, s)
            if not last:
                send_parts(it + 1, s)
            sums_copy(it, s).wait_send()
            for l in range(layers):
                grad_copy(it, s, l).wait_send()

    pl.semaphore_wait(barrier, cells)
    for s in range(2):
        for l in range(layers):
            start_halo(prior, 0, s, l)
    for s in range(2):
        acc[...] = jnp.zeros_like(acc)

        @pl.loop(0, layers)
        def _(l, s=s):
            load(s, l).wait()
            value = raw[s, l]
            rounded = value.astype(jnp.bfloat16)
            high[s, l] = rounded
            low[s, l] = (value - rounded.astype(jnp.float32)).astype(jnp.bfloat16)
            high_t[s, l] = high[s, l].T
            low_t[s, l] = low[s, l].T
            predict(s, l, prior[s, l])

        send_parts(0, s)

    step(prior, 0, ITERS == 1)
    if ITERS > 2:
        @pl.loop(1, ITERS - 1)
        def _(it):
            step(out, it, False)
    if ITERS > 1:
        step(out, ITERS - 1, True)


def body(sens, observed, noise, survey_ids, data_perturb, prior):
    cells = lax.axis_size("cell")
    models, layers, layer_cells = prior.shape[1:]
    stations = observed.shape[1]
    tiles = stations // LANES
    assert models == 8 and stations % LANES == 0
    assert lax.axis_size("dp") == 2
    f32, bf16 = jnp.float32, jnp.bfloat16
    field = (2, layers, models, layer_cells)
    vmem = pl.BlockSpec(memory_space=pltpu.VMEM)
    dma = pltpu.SemaphoreType.DMA
    out = pl.pallas_call(
        functools.partial(kernel, cells),
        out_shape=jax.ShapeDtypeStruct(field, f32),
        in_specs=[pl.BlockSpec(memory_space=pl.ANY)] + [vmem] * 5,
        out_specs=vmem,
        scratch_shapes=[
            pltpu.VMEM((2, layers, stations, layer_cells), f32),
            pltpu.VMEM((2, layers, stations, layer_cells), bf16),
            pltpu.VMEM((2, layers, stations, layer_cells), bf16),
            pltpu.VMEM((2, layers, layer_cells, stations), bf16),
            pltpu.VMEM((2, layers, layer_cells, stations), bf16),
            pltpu.VMEM(field, f32),
            pltpu.VMEM((2, models, layer_cells), f32),
            pltpu.VMEM((ITERS, 2, models, layer_cells), f32),
            pltpu.VMEM((ITERS, 2, models, layer_cells), f32),
            pltpu.VMEM((2 * models, stations), f32),
            pltpu.VMEM((ITERS, 2, cells, models, stations), f32),
            pltpu.VMEM((2, models, stations), f32),
            pltpu.VMEM((2, models, stations), f32),
            pltpu.VMEM((2, models, stations), f32),
            pltpu.VMEM((2, models, LANES), f32),
            pltpu.VMEM((ITERS, 2, models, LANES), f32),
            pltpu.VMEM((ITERS, 2, models, LANES), f32),
            pltpu.VMEM((2, 2 * models, stations), bf16),
            pltpu.VMEM(field, f32),
            pltpu.VMEM((ITERS,) + field, f32),
            dma((2, layers)),
            dma((2, 2)),
            dma((ITERS, 2, 2)),
            dma((2,)),
            dma((ITERS, 2)),
            dma((2,)),
            dma((ITERS, 2)),
            dma((2, layers)),
            dma((ITERS, 2, layers)),
        ],
        compiler_params=pltpu.CompilerParams(
            collective_id=0, has_side_effects=True, vmem_limit_bytes=60 * 1024 * 1024
        ),
    )(sens, observed, noise, survey_ids, data_perturb, prior.transpose(0, 2, 1, 3))
    return out.transpose(0, 2, 1, 3)


def solution(mesh):
    return jax.shard_map(
        body,
        mesh=mesh,
        in_specs=(
            P(None, ("slab", "dp"), "cell"),
            P(None, ("slab", "dp")),
            P(None, ("slab", "dp")),
            P(None, ("slab", "dp")),
            P(None, None, ("slab", "dp")),
            P(None, "slab", "cell", None),
        ),
        out_specs=P(None, "slab", "cell", None),
        check_vma=False,
    )
```

```python
import functools

import jax
import jax.numpy as jnp
from jax import lax
from jax.experimental import pallas as pl
from jax.experimental.pallas import tpu as pltpu
from jax.sharding import PartitionSpec as P

NX = 32
NZ = 32
NSURV = 8
ITERS = 4
LANES = 128
MODELS = 8
PARTS = 2

nu_value = 4.0
step_size = 0.5
couple_weight = 0.02
prior_weight = 0.1

MESH = pl.DeviceIdType.MESH


def split_rows(value):
    high = value.astype(jnp.bfloat16).astype(jnp.float32)
    return jnp.concatenate([high, value - high], axis=0).astype(jnp.bfloat16)


def fold_rows(value):
    half = value.shape[0] // 2
    return value[:half] + value[half:]


def cross_gradients(first, second, masks, layer_cells, z_on):
    along_x, along_y = masks

    def differences(field, deeper):
        diff_x = (pltpu.roll(field, layer_cells - 1, 1) - field) * along_x
        diff_y = (pltpu.roll(field, layer_cells - NX, 1) - field) * along_y
        return diff_x, diff_y, (deeper - field) * z_on

    a = differences(*first)
    b = differences(*second)
    tx = a[1] * b[2] - a[2] * b[1]
    ty = a[2] * b[0] - a[0] * b[2]
    tz = a[0] * b[1] - a[1] * b[0]
    scaling = 2.0 / (1.0 + tx * tx + ty * ty + tz * tz)
    sx = scaling * along_x
    sy = scaling * along_y
    sz = scaling * z_on
    return (
        (sx * (b[1] * tz - b[2] * ty), sy * (b[2] * tx - b[0] * tz), sz * (b[0] * ty - b[1] * tx)),
        (sx * (ty * a[2] - tz * a[1]), sy * (tz * a[0] - tx * a[2]), sz * (tx * a[1] - ty * a[0])),
    )


def kernel(
    cells, layers, sens, observed_in, noise_in, ids_in, perturb_in, prior_in, result,
    observed, noise, survey_ids, perturb, prior_raw, prior, out, raw, high, low, high_t, low_t, base, carry_z, halo_up, halo_dn, acc, gather, target, per_noise, resids,
    count_tile, sums_mine, sums_other, rows, grad_mine, grad_other,
    input_sem, load_sem, halo_send, halo_recv, part_send, part_recv, sums_send, sums_recv, grad_send, grad_recv,
):
    stations = observed.shape[1]
    layer_cells = prior.shape[3]
    blocks = layer_cells // LANES
    tiles = stations // LANES
    slab = lax.axis_index("slab")
    me = lax.axis_index("cell")
    dp = lax.axis_index("dp")
    partner = 1 - dp
    width = layer_cells // PARTS
    order = sorted(range(layers), key=lambda l: 0 < l < layers - 1)
    pieces = [(l, slice(h * width, (h + 1) * width)) for l in order for h in range(PARTS)]

    def load(s, l):
        return pltpu.make_async_copy(
            sens.at[s, :, pl.ds(pl.multiple_of(l * layer_cells, LANES), layer_cells)], raw.at[s, l],
            load_sem.at[s, l],
        )

    inputs = [
        pltpu.make_async_copy(source, kept, input_sem.at[i])
        for i, (source, kept) in enumerate((
            (prior_in, prior_raw), (observed_in, observed), (noise_in, noise), (ids_in, survey_ids),
            (perturb_in, perturb),
        ))
    ]
    for copy in inputs:
        copy.start()
    for n in range(min(2, 2 * layers)):
        load(n // layers, n % layers).start()

    barrier = pltpu.get_barrier_semaphore()
    pl.semaphore_signal(barrier, inc=1, device_id=(slab, me, partner), device_id_type=MESH)
    for k in range(1, cells):
        there = lax.rem(me + k, cells)
        pl.semaphore_signal(barrier, inc=1, device_id=(slab, there, dp), device_id_type=MESH)

    position = lax.broadcasted_iota(jnp.int32, (1, layer_cells), 1)
    masks = (
        (lax.rem(position, NX) < NX - 1).astype(jnp.float32),
        (position < layer_cells - NX).astype(jnp.float32),
    )
    lane = lax.broadcasted_iota(jnp.int32, (8, LANES), 1)

    @pl.when(me == cells - 1)
    def _():
        halo_up[...] = jnp.zeros_like(halo_up)

    @pl.when(me == 0)
    def _():
        halo_dn[...] = jnp.zeros_like(halo_dn)

    def rows_of(l, j):
        return pl.ds(j * layers + l, MODELS, stride=blocks * layers)

    for copy in inputs:
        copy.wait()
    for s in range(2):
        for l in range(layers):
            for j in range(blocks):
                prior[s, l, :, j * LANES : (j + 1) * LANES] = prior_raw[s, rows_of(l, j), :]

    def ids_at(s, t):
        return jnp.broadcast_to(survey_ids[s : s + 1, t * LANES : (t + 1) * LANES], (8, LANES))

    def by_survey(s, values, offset):
        total = jnp.zeros((8, LANES), jnp.float32)
        ids = [ids_at(s, t) for t in range(tiles)]
        for j in range(NSURV):
            one = jnp.where(ids[0] == j, values[0], 0.0)
            for t in range(1, tiles):
                one = one + jnp.where(ids[t] == j, values[t], 0.0)
            total = jnp.where(lane == j + offset, jnp.sum(one, axis=1, keepdims=True), total)
        return total

    for s in range(2):
        count_tile[s] = by_survey(s, [jnp.ones((8, LANES), jnp.float32)] * tiles, NSURV)
        scale = noise[s : s + 1]
        target[s] = observed[s : s + 1] + scale * perturb[s]
        per_noise[s] = jnp.broadcast_to(1.0 / scale, per_noise.shape[1:])

    def halo_copy(source, it, s, up):
        return pltpu.make_async_remote_copy(
            src_ref=source.at[s, 0 if up else layers - 1],
            dst_ref=(halo_up if up else halo_dn).at[it, s],
            send_sem=halo_send.at[s, 0 if up else 1],
            recv_sem=halo_recv.at[it, s, 0 if up else 1],
            device_id=(slab, jnp.maximum(me - 1, 0) if up else jnp.minimum(me + 1, cells - 1), dp),
            device_id_type=MESH,
        )

    def start_halo(source, it, s, l):
        if l == 0:
            @pl.when(me > 0)
            def _():
                halo_copy(source, it, s, True).start()

        if l == layers - 1:
            @pl.when(me < cells - 1)
            def _():
                halo_copy(source, it, s, False).start()

    def wait_halo_sent(source, it, s):
        @pl.when(me > 0)
        def _():
            halo_copy(source, it, s, True).wait_send()

        @pl.when(me < cells - 1)
        def _():
            halo_copy(source, it, s, False).wait_send()

    def wait_halos_here(source, it):
        @pl.when(me < cells - 1)
        def _():
            for s in range(2):
                halo_copy(source, it, s, True).wait_recv()

        @pl.when(me > 0)
        def _():
            for s in range(2):
                halo_copy(source, it, s, False).wait_recv()

    def send_parts(it, s, total):
        gather[it, s, me] = fold_rows(total)
        for k in range(1, cells):
            pltpu.make_async_remote_copy(
                src_ref=gather.at[it, s, me], dst_ref=gather.at[it, s, me],
                send_sem=part_send.at[s], recv_sem=part_recv.at[it, s],
                device_id=(slab, lax.rem(me + k, cells), dp), device_id_type=MESH,
            ).start()

    def wait_parts_sent(it, s):
        sent = gather.at[it, s, pl.ds(0, cells - 1)]
        pltpu.make_async_copy(sent, sent, part_send.at[s]).wait()

    def sums_copy(it, s):
        return pltpu.make_async_remote_copy(
            src_ref=sums_mine.at[it, s], dst_ref=sums_other.at[it, s],
            send_sem=sums_send.at[s], recv_sem=sums_recv.at[it, s],
            device_id=(slab, me, partner), device_id_type=MESH,
        )

    def residuals(it, s):
        got = gather.at[it, s, pl.ds(0, cells - 1)]
        pltpu.make_async_copy(got, got, part_recv.at[it, s]).wait()
        squares = []
        for t in range(tiles):
            span = slice(t * LANES, (t + 1) * LANES)
            predicted = gather[it, s, 0, :, span]
            for c in range(1, cells):
                predicted = predicted + gather[it, s, c, :, span]
            resid = (predicted - target[s, :, span]) * per_noise[s, :, span]
            resids[s, :, span] = resid
            squares.append(resid * resid)
        sums_mine[it, s] = by_survey(s, squares, 0) + count_tile[s]
        sums_copy(it, s).start()

    def weigh(it, s):
        sums_copy(it, s).wait_recv()
        sums = sums_mine[it, s] + sums_other[it, s]
        counts = pltpu.roll(sums, LANES - NSURV, 1)
        per_root = lax.rsqrt((sums + 1.0) / (counts + 1.0))
        columns = [jnp.broadcast_to(per_root[:, j : j + 1], (8, LANES)) for j in range(NSURV)]
        for t in range(tiles):
            span = slice(t * LANES, (t + 1) * LANES)
            ids = ids_at(s, t)
            per_scale = columns[0]
            for j in range(1, NSURV):
                per_scale = jnp.where(ids == j, columns[j], per_scale)
            whitened = resids[s, :, span] * per_scale
            factor = (
                (nu_value + 1.0) * whitened * (per_noise[s, :, span] * per_scale)
                / (nu_value + whitened * whitened)
            )
            rows[s, :, span] = split_rows(factor)

    def grad_copy(it, s, p):
        return pltpu.make_async_remote_copy(
            src_ref=grad_mine.at[s, p], dst_ref=grad_other.at[it, s, p],
            send_sem=grad_send.at[s, p], recv_sem=grad_recv.at[it, s, p],
            device_id=(slab, me, partner), device_id_type=MESH,
        )

    def gradient(it, s, beside):
        factor = rows[s]

        def finish(p, product):
            grad_mine[s, p] = fold_rows(product)
            grad_copy(it, s, p).start()

        held = None
        for p, (l, span) in enumerate(pieces):
            product = jnp.dot(factor, high[s, l, :, span], preferred_element_type=jnp.float32)
            product = product + jnp.dot(factor, low[s, l, :, span], preferred_element_type=jnp.float32)
            beside(p)
            if held is not None:
                finish(p - 1, held)
            held = product
        finish(len(pieces) - 1, held)

    def predict(s, l, span, value):
        model = split_rows(value)
        product = jnp.dot(model, high_t[s, l, span], preferred_element_type=jnp.float32)
        return product + jnp.dot(model, low_t[s, l, span], preferred_element_type=jnp.float32)

    def couple(source, it, l):
        if l == layers - 1:
            wait_halos_here(source, it)
        z_on = (me * layers + l < NZ - 1).astype(jnp.float32)
        first, second = [
            (source[s, l], source[s, l + 1] if l < layers - 1 else halo_up[it, s]) for s in range(2)
        ]
        both = cross_gradients(first, second, masks, layer_cells, z_on)
        for s in range(2):
            gx, gy, gz = both[s]
            total = pltpu.roll(gx, 1, 1) - gx + (pltpu.roll(gy, NX, 1) - gy) - gz
            if l > 0:
                total = total + carry_z[s]
            carry_z[s] = gz
            field = source[s, l]
            base[s, l] = field - step_size * (
                couple_weight * total + prior_weight * (field - prior[s, l])
            )
        if l == layers - 1:
            z_on = (me > 0).astype(jnp.float32)
            first, second = [(halo_dn[it, s], source[s, 0]) for s in range(2)]
            both = cross_gradients(first, second, masks, layer_cells, z_on)
            for s in range(2):
                base[s, 0] -= step_size * couple_weight * both[s][2]

    def advance(source, it, s, last):
        wait_halo_sent(source, it, s)
        total = jnp.zeros((2 * MODELS, stations), jnp.float32)
        for p, (l, span) in enumerate(pieces):
            grad_copy(it, s, p).wait_recv()
            value = base[s, l, :, span] - step_size * (grad_mine[s, p] + grad_other[it, s, p])
            if last:
                for j in range(width // LANES):
                    result[s, rows_of(l, span.start // LANES + j), :] = value[:, j * LANES : (j + 1) * LANES]
            else:
                out[s, l, :, span] = value
                if p % PARTS == PARTS - 1:
                    start_halo(out, it + 1, s, l)
                total = total + predict(s, l, span, value)
        wait_parts_sent(it, s)
        if not last:
            send_parts(it + 1, s, total)
        sums_copy(it, s).wait_send()
        for p in range(len(pieces)):
            grad_copy(it, s, p).wait_send()

    def step(source, it, last):
        residuals(it, 0)
        weigh(it, 0)

        def beside(p):
            if p % PARTS == 0:
                couple(source, it, p // PARTS)

        gradient(it, 0, beside)
        advance(source, it, 0, last)
        residuals(it, 1)
        weigh(it, 1)
        gradient(it, 1, lambda p: None)
        advance(source, it, 1, last)

    pl.semaphore_wait(barrier, cells)
    for s in range(2):
        for l in range(layers):
            start_halo(prior, 0, s, l)
    for s in range(2):
        acc[...] = jnp.zeros_like(acc)

        @pl.loop(0, layers)
        def _(l, s=s):
            load(s, l).wait()
            later = s * layers + l + 2

            @pl.when(later < 2 * layers)
            def _():
                load(later // layers, lax.rem(later, layers)).start()

            value = raw[s, l]
            rounded = value.astype(jnp.bfloat16)
            high[s, l] = rounded
            low[s, l] = (value - rounded.astype(jnp.float32)).astype(jnp.bfloat16)
            high_t[s, l] = high[s, l].T
            low_t[s, l] = low[s, l].T
            acc[...] += predict(s, l, slice(0, layer_cells), prior[s, l])

        send_parts(0, s, acc[...])

    step(prior, 0, ITERS == 1)
    if ITERS > 2:
        @pl.loop(1, ITERS - 1)
        def _(it):
            step(out, it, False)
    if ITERS > 1:
        step(out, ITERS - 1, True)


def body(sens, observed, noise, survey_ids, data_perturb, prior):
    cells = lax.axis_size("cell")
    models, layers, layer_cells = prior.shape[1:]
    stations = observed.shape[1]
    tiles = stations // LANES
    pieces, width = layers * PARTS, layer_cells // PARTS
    assert models == MODELS and stations % LANES == 0 and width % LANES == 0
    assert lax.axis_size("dp") == 2
    f32, bf16 = jnp.float32, jnp.bfloat16
    field = (2, layers, models, layer_cells)
    blocks = layer_cells // LANES
    flat = (2, models * blocks * layers, LANES)
    vmem = pl.BlockSpec(memory_space=pltpu.VMEM)
    dma = pltpu.SemaphoreType.DMA
    prior = prior.reshape(2, models, layers, blocks, LANES).transpose(0, 1, 3, 2, 4).reshape(flat)
    out = pl.pallas_call(
        functools.partial(kernel, cells, layers),
        out_shape=jax.ShapeDtypeStruct(flat, f32),
        in_specs=[pl.BlockSpec(memory_space=pl.ANY)] * 6,
        out_specs=vmem,
        scratch_shapes=[
            pltpu.VMEM((2, stations), f32),
            pltpu.VMEM((2, stations), f32),
            pltpu.VMEM((2, stations), jnp.int32),
            pltpu.VMEM((2, models, stations), f32),
            pltpu.VMEM(flat, f32),
            pltpu.VMEM(field, f32),
            pltpu.VMEM(field, f32),
            pltpu.VMEM((2, layers, stations, layer_cells), f32),
            pltpu.VMEM((2, layers, stations, layer_cells), bf16),
            pltpu.VMEM((2, layers, stations, layer_cells), bf16),
            pltpu.VMEM((2, layers, layer_cells, stations), bf16),
            pltpu.VMEM((2, layers, layer_cells, stations), bf16),
            pltpu.VMEM(field, f32),
            pltpu.VMEM((2, models, layer_cells), f32),
            pltpu.VMEM((ITERS, 2, models, layer_cells), f32),
            pltpu.VMEM((ITERS, 2, models, layer_cells), f32),
            pltpu.VMEM((2 * models, stations), f32),
            pltpu.VMEM((ITERS, 2, cells, models, stations), f32),
            pltpu.VMEM((2, models, stations), f32),
            pltpu.VMEM((2, models, stations), f32),
            pltpu.VMEM((2, models, stations), f32),
            pltpu.VMEM((2, models, LANES), f32),
            pltpu.VMEM((ITERS, 2, models, LANES), f32),
            pltpu.VMEM((ITERS, 2, models, LANES), f32),
            pltpu.VMEM((2, 2 * models, stations), bf16),
            pltpu.VMEM((2, pieces, models, width), f32),
            pltpu.VMEM((ITERS, 2, pieces, models, width), f32),
            dma((5,)),
            dma((2, layers)),
            dma((2, 2)),
            dma((ITERS, 2, 2)),
            dma((2,)),
            dma((ITERS, 2)),
            dma((2,)),
            dma((ITERS, 2)),
            dma((2, pieces)),
            dma((ITERS, 2, pieces)),
        ],
        compiler_params=pltpu.CompilerParams(
            collective_id=0, has_side_effects=True, vmem_limit_bytes=57000 * 1024
        ),
    )(sens, observed, noise, survey_ids, data_perturb, prior)
    out = out.reshape(2, models, blocks, layers, LANES).transpose(0, 1, 3, 2, 4)
    return out.reshape(2, models, layers, layer_cells)


def solution(mesh):
    return jax.shard_map(
        body,
        mesh=mesh,
        in_specs=(
            P(None, ("slab", "dp"), "cell"),
            P(None, ("slab", "dp")),
            P(None, ("slab", "dp")),
            P(None, ("slab", "dp")),
            P(None, None, ("slab", "dp")),
            P(None, "slab", "cell", None),
        ),
        out_specs=P(None, "slab", "cell", None),
        check_vma=False,
    )
```

```python
import functools

import jax
import jax.numpy as jnp
from jax import lax
from jax.experimental import pallas as pl
from jax.experimental.pallas import tpu as pltpu
from jax.sharding import PartitionSpec as P

NX = 32
NZ = 32
NSURV = 8
ITERS = 4
LANES = 128
MODELS = 8
PARTS = 1

nu_value = 4.0
step_size = 0.5
couple_weight = 0.02
prior_weight = 0.1

MESH = pl.DeviceIdType.MESH


def split_rows(value):
    high = value.astype(jnp.bfloat16).astype(jnp.float32)
    return jnp.concatenate([high, value - high], axis=0).astype(jnp.bfloat16)


def fold_rows(value):
    half = value.shape[0] // 2
    return value[:half] + value[half:]


def cross_gradients(first, second, masks, layer_cells, z_on):
    along_x, along_y = masks

    def differences(field, deeper):
        diff_x = (pltpu.roll(field, layer_cells - 1, 1) - field) * along_x
        diff_y = (pltpu.roll(field, layer_cells - NX, 1) - field) * along_y
        return diff_x, diff_y, (deeper - field) * z_on

    a = differences(*first)
    b = differences(*second)
    tx = a[1] * b[2] - a[2] * b[1]
    ty = a[2] * b[0] - a[0] * b[2]
    tz = a[0] * b[1] - a[1] * b[0]
    scaling = 2.0 / (1.0 + tx * tx + ty * ty + tz * tz)
    sx = scaling * along_x
    sy = scaling * along_y
    sz = scaling * z_on
    return (
        (sx * (b[1] * tz - b[2] * ty), sy * (b[2] * tx - b[0] * tz), sz * (b[0] * ty - b[1] * tx)),
        (sx * (ty * a[2] - tz * a[1]), sy * (tz * a[0] - tx * a[2]), sz * (tx * a[1] - ty * a[0])),
    )


def kernel(
    cells, layers, sens, observed_in, noise_in, ids_in, perturb_in, prior_in, result_out,
    observed, noise, survey_ids, perturb, prior_raw, prior, out, result, raw, high, low, high_t, low_t, base, carry_z, halo_up, halo_dn, acc, gather, target, per_noise, resids,
    count_tile, sums_mine, sums_other, rows, grad_mine, grad_other,
    input_sem, result_sem, load_sem, halo_send, halo_recv, part_send, part_recv, sums_send, sums_recv, grad_send, grad_recv,
):
    stations = observed.shape[1]
    layer_cells = prior.shape[3]
    blocks = layer_cells // LANES
    tiles = stations // LANES
    slab = lax.axis_index("slab")
    me = lax.axis_index("cell")
    dp = lax.axis_index("dp")
    partner = 1 - dp
    width = layer_cells // PARTS
    order = sorted(range(layers), key=lambda l: 0 < l < layers - 1)
    pieces = [(l, slice(h * width, (h + 1) * width)) for l in order for h in range(PARTS)]

    def load(s, l):
        return pltpu.make_async_copy(
            sens.at[s, :, pl.ds(pl.multiple_of(l * layer_cells, LANES), layer_cells)], raw.at[s, l],
            load_sem.at[s, l],
        )

    inputs = [
        pltpu.make_async_copy(source, kept, input_sem.at[i])
        for i, (source, kept) in enumerate((
            (prior_in, prior_raw), (observed_in, observed), (noise_in, noise), (ids_in, survey_ids),
            (perturb_in, perturb),
        ))
    ]
    for copy in inputs:
        copy.start()
    for n in range(min(2, 2 * layers)):
        load(n // layers, n % layers).start()

    barrier = pltpu.get_barrier_semaphore()
    pl.semaphore_signal(barrier, inc=1, device_id=(slab, me, partner), device_id_type=MESH)
    for k in range(1, cells):
        there = lax.rem(me + k, cells)
        pl.semaphore_signal(barrier, inc=1, device_id=(slab, there, dp), device_id_type=MESH)

    position = lax.broadcasted_iota(jnp.int32, (1, layer_cells), 1)
    masks = (
        (lax.rem(position, NX) < NX - 1).astype(jnp.float32),
        (position < layer_cells - NX).astype(jnp.float32),
    )
    lane = lax.broadcasted_iota(jnp.int32, (8, LANES), 1)

    @pl.when(me == cells - 1)
    def _():
        halo_up[...] = jnp.zeros_like(halo_up)

    @pl.when(me == 0)
    def _():
        halo_dn[...] = jnp.zeros_like(halo_dn)

    def rows_of(l, j):
        return pl.ds(j * layers + l, MODELS, stride=blocks * layers)

    for copy in inputs:
        copy.wait()
    for s in range(2):
        for l in range(layers):
            for j in range(blocks):
                prior[s, l, :, j * LANES : (j + 1) * LANES] = prior_raw[s, rows_of(l, j), :]

    def ids_at(s, t):
        return jnp.broadcast_to(survey_ids[s : s + 1, t * LANES : (t + 1) * LANES], (8, LANES))

    def by_survey(s, values, offset):
        total = jnp.zeros((8, LANES), jnp.float32)
        ids = [ids_at(s, t) for t in range(tiles)]
        for j in range(NSURV):
            one = jnp.where(ids[0] == j, values[0], 0.0)
            for t in range(1, tiles):
                one = one + jnp.where(ids[t] == j, values[t], 0.0)
            total = jnp.where(lane == j + offset, jnp.sum(one, axis=1, keepdims=True), total)
        return total

    for s in range(2):
        count_tile[s] = by_survey(s, [jnp.ones((8, LANES), jnp.float32)] * tiles, NSURV)
        scale = noise[s : s + 1]
        target[s] = observed[s : s + 1] + scale * perturb[s]
        per_noise[s] = jnp.broadcast_to(1.0 / scale, per_noise.shape[1:])

    def halo_copy(source, it, s, up):
        return pltpu.make_async_remote_copy(
            src_ref=source.at[s, 0 if up else layers - 1],
            dst_ref=(halo_up if up else halo_dn).at[it, s],
            send_sem=halo_send.at[s, 0 if up else 1],
            recv_sem=halo_recv.at[it, s, 0 if up else 1],
            device_id=(slab, jnp.maximum(me - 1, 0) if up else jnp.minimum(me + 1, cells - 1), dp),
            device_id_type=MESH,
        )

    def start_halo(source, it, s, l):
        if l == 0:
            @pl.when(me > 0)
            def _():
                halo_copy(source, it, s, True).start()

        if l == layers - 1:
            @pl.when(me < cells - 1)
            def _():
                halo_copy(source, it, s, False).start()

    def wait_halo_sent(source, it, s):
        @pl.when(me > 0)
        def _():
            halo_copy(source, it, s, True).wait_send()

        @pl.when(me < cells - 1)
        def _():
            halo_copy(source, it, s, False).wait_send()

    def wait_halos_here(source, it):
        @pl.when(me < cells - 1)
        def _():
            for s in range(2):
                halo_copy(source, it, s, True).wait_recv()

        @pl.when(me > 0)
        def _():
            for s in range(2):
                halo_copy(source, it, s, False).wait_recv()

    def send_parts(it, s, total):
        gather[it, s, me] = fold_rows(total)
        for k in range(1, cells):
            pltpu.make_async_remote_copy(
                src_ref=gather.at[it, s, me], dst_ref=gather.at[it, s, me],
                send_sem=part_send.at[s], recv_sem=part_recv.at[it, s],
                device_id=(slab, lax.rem(me + k, cells), dp), device_id_type=MESH,
            ).start()

    def wait_parts_sent(it, s):
        sent = gather.at[it, s, pl.ds(0, cells - 1)]
        pltpu.make_async_copy(sent, sent, part_send.at[s]).wait()

    def sums_copy(it, s):
        return pltpu.make_async_remote_copy(
            src_ref=sums_mine.at[it, s], dst_ref=sums_other.at[it, s],
            send_sem=sums_send.at[s], recv_sem=sums_recv.at[it, s],
            device_id=(slab, me, partner), device_id_type=MESH,
        )

    def residuals(it, s):
        got = gather.at[it, s, pl.ds(0, cells - 1)]
        pltpu.make_async_copy(got, got, part_recv.at[it, s]).wait()
        squares = []
        for t in range(tiles):
            span = slice(t * LANES, (t + 1) * LANES)
            predicted = gather[it, s, 0, :, span]
            for c in range(1, cells):
                predicted = predicted + gather[it, s, c, :, span]
            resid = (predicted - target[s, :, span]) * per_noise[s, :, span]
            resids[s, :, span] = resid
            squares.append(resid * resid)
        sums_mine[it, s] = by_survey(s, squares, 0) + count_tile[s]
        sums_copy(it, s).start()

    def weigh(it, s):
        sums_copy(it, s).wait_recv()
        sums = sums_mine[it, s] + sums_other[it, s]
        counts = pltpu.roll(sums, LANES - NSURV, 1)
        per_root = lax.rsqrt((sums + 1.0) / (counts + 1.0))
        columns = [jnp.broadcast_to(per_root[:, j : j + 1], (8, LANES)) for j in range(NSURV)]
        for t in range(tiles):
            span = slice(t * LANES, (t + 1) * LANES)
            ids = ids_at(s, t)
            per_scale = columns[0]
            for j in range(1, NSURV):
                per_scale = jnp.where(ids == j, columns[j], per_scale)
            whitened = resids[s, :, span] * per_scale
            factor = (
                (nu_value + 1.0) * whitened * (per_noise[s, :, span] * per_scale)
                / (nu_value + whitened * whitened)
            )
            rows[s, :, span] = split_rows(factor)

    def grad_copy(it, s, p):
        return pltpu.make_async_remote_copy(
            src_ref=grad_mine.at[s, p], dst_ref=grad_other.at[it, s, p],
            send_sem=grad_send.at[s, p], recv_sem=grad_recv.at[it, s, p],
            device_id=(slab, me, partner), device_id_type=MESH,
        )

    def gradient(it, s, beside):
        factor = rows[s]

        def finish(p, product):
            grad_mine[s, p] = fold_rows(product)
            grad_copy(it, s, p).start()

        held = None
        for p, (l, span) in enumerate(pieces):
            product = jnp.dot(factor, high[s, l, :, span], preferred_element_type=jnp.float32)
            product = product + jnp.dot(factor, low[s, l, :, span], preferred_element_type=jnp.float32)
            beside(p)
            if held is not None:
                finish(p - 1, held)
            held = product
        finish(len(pieces) - 1, held)

    def predict(s, l, span, value):
        model = split_rows(value)
        product = jnp.dot(model, high_t[s, l, span], preferred_element_type=jnp.float32)
        return product + jnp.dot(model, low_t[s, l, span], preferred_element_type=jnp.float32)

    def couple(source, it, l):
        if l == layers - 1:
            wait_halos_here(source, it)
        z_on = (me * layers + l < NZ - 1).astype(jnp.float32)
        first, second = [
            (source[s, l], source[s, l + 1] if l < layers - 1 else halo_up[it, s]) for s in range(2)
        ]
        both = cross_gradients(first, second, masks, layer_cells, z_on)
        for s in range(2):
            gx, gy, gz = both[s]
            total = pltpu.roll(gx, 1, 1) - gx + (pltpu.roll(gy, NX, 1) - gy) - gz
            if l > 0:
                total = total + carry_z[s]
            carry_z[s] = gz
            field = source[s, l]
            base[s, l] = field - step_size * (
                couple_weight * total + prior_weight * (field - prior[s, l])
            )

    def couple_below(source, it):
        z_on = (me > 0).astype(jnp.float32)
        first, second = [(halo_dn[it, s], source[s, 0]) for s in range(2)]
        both = cross_gradients(first, second, masks, layer_cells, z_on)
        for s in range(2):
            base[s, 0] -= step_size * couple_weight * both[s][2]

    def advance(source, it, s, last):
        wait_halo_sent(source, it, s)
        total = jnp.zeros((2 * MODELS, stations), jnp.float32)
        for p, (l, span) in enumerate(pieces):
            grad_copy(it, s, p).wait_recv()
            value = base[s, l, :, span] - step_size * (grad_mine[s, p] + grad_other[it, s, p])
            if last:
                for j in range(width // LANES):
                    result[s, rows_of(l, span.start // LANES + j), :] = value[:, j * LANES : (j + 1) * LANES]
            else:
                out[s, l, :, span] = value
                if p % PARTS == PARTS - 1:
                    start_halo(out, it + 1, s, l)
                total = total + predict(s, l, span, value)
        wait_parts_sent(it, s)
        if not last:
            send_parts(it + 1, s, total)
        if last:
            pltpu.make_async_copy(result.at[s], result_out.at[s], result_sem.at[s]).start()
        sums_copy(it, s).wait_send()
        for p in range(len(pieces)):
            grad_copy(it, s, p).wait_send()

    def step(source, it, last):
        residuals(it, 0)
        for l in range(layers - 1):
            couple(source, it, l)
        weigh(it, 0)

        def beside(p):
            if p == max(len(pieces) - 4, 0):
                couple(source, it, layers - 1)
            if p == len(pieces) - 2:
                couple_below(source, it)

        gradient(it, 0, beside)
        advance(source, it, 0, last)
        residuals(it, 1)
        weigh(it, 1)
        gradient(it, 1, lambda p: None)
        advance(source, it, 1, last)

    pl.semaphore_wait(barrier, cells)
    for s in range(2):
        for l in range(layers):
            start_halo(prior, 0, s, l)
    for s in range(2):
        acc[...] = jnp.zeros_like(acc)

        @pl.loop(0, layers)
        def _(l, s=s):
            load(s, l).wait()
            later = s * layers + l + 2

            @pl.when(later < 2 * layers)
            def _():
                load(later // layers, lax.rem(later, layers)).start()

            value = raw[s, l]
            rounded = value.astype(jnp.bfloat16)
            high[s, l] = rounded
            low[s, l] = (value - rounded.astype(jnp.float32)).astype(jnp.bfloat16)
            high_t[s, l] = high[s, l].T
            low_t[s, l] = low[s, l].T
            acc[...] += predict(s, l, slice(0, layer_cells), prior[s, l])

        send_parts(0, s, acc[...])

    step(prior, 0, ITERS == 1)
    if ITERS > 2:
        @pl.loop(1, ITERS - 1)
        def _(it):
            step(out, it, False)
    if ITERS > 1:
        step(out, ITERS - 1, True)
    for s in range(2):
        pltpu.make_async_copy(result.at[s], result_out.at[s], result_sem.at[s]).wait()


def body(sens, observed, noise, survey_ids, data_perturb, prior):
    cells = lax.axis_size("cell")
    models, layers, layer_cells = prior.shape[1:]
    stations = observed.shape[1]
    tiles = stations // LANES
    pieces, width = layers * PARTS, layer_cells // PARTS
    assert models == MODELS and stations % LANES == 0 and width % LANES == 0
    assert lax.axis_size("dp") == 2
    f32, bf16 = jnp.float32, jnp.bfloat16
    field = (2, layers, models, layer_cells)
    blocks = layer_cells // LANES
    flat = (2, models * blocks * layers, LANES)
    vmem = pl.BlockSpec(memory_space=pltpu.VMEM)
    dma = pltpu.SemaphoreType.DMA
    prior = prior.reshape(2, models, layers, blocks, LANES).transpose(0, 1, 3, 2, 4).reshape(flat)
    out = pl.pallas_call(
        functools.partial(kernel, cells, layers),
        out_shape=jax.ShapeDtypeStruct(flat, f32),
        in_specs=[pl.BlockSpec(memory_space=pl.ANY)] * 6,
        out_specs=pl.BlockSpec(memory_space=pl.ANY),
        scratch_shapes=[
            pltpu.VMEM((2, stations), f32),
            pltpu.VMEM((2, stations), f32),
            pltpu.VMEM((2, stations), jnp.int32),
            pltpu.VMEM((2, models, stations), f32),
            pltpu.VMEM(flat, f32),
            pltpu.VMEM(field, f32),
            pltpu.VMEM(field, f32),
            pltpu.VMEM(flat, f32),
            pltpu.VMEM((2, layers, stations, layer_cells), f32),
            pltpu.VMEM((2, layers, stations, layer_cells), bf16),
            pltpu.VMEM((2, layers, stations, layer_cells), bf16),
            pltpu.VMEM((2, layers, layer_cells, stations), bf16),
            pltpu.VMEM((2, layers, layer_cells, stations), bf16),
            pltpu.VMEM(field, f32),
            pltpu.VMEM((2, models, layer_cells), f32),
            pltpu.VMEM((ITERS, 2, models, layer_cells), f32),
            pltpu.VMEM((ITERS, 2, models, layer_cells), f32),
            pltpu.VMEM((2 * models, stations), f32),
            pltpu.VMEM((ITERS, 2, cells, models, stations), f32),
            pltpu.VMEM((2, models, stations), f32),
            pltpu.VMEM((2, models, stations), f32),
            pltpu.VMEM((2, models, stations), f32),
            pltpu.VMEM((2, models, LANES), f32),
            pltpu.VMEM((ITERS, 2, models, LANES), f32),
            pltpu.VMEM((ITERS, 2, models, LANES), f32),
            pltpu.VMEM((2, 2 * models, stations), bf16),
            pltpu.VMEM((2, pieces, models, width), f32),
            pltpu.VMEM((ITERS, 2, pieces, models, width), f32),
            dma((5,)),
            dma((2,)),
            dma((2, layers)),
            dma((2, 2)),
            dma((ITERS, 2, 2)),
            dma((2,)),
            dma((ITERS, 2)),
            dma((2,)),
            dma((ITERS, 2)),
            dma((2, pieces)),
            dma((ITERS, 2, pieces)),
        ],
        compiler_params=pltpu.CompilerParams(
            collective_id=0, has_side_effects=True, vmem_limit_bytes=57000 * 1024
        ),
    )(sens, observed, noise, survey_ids, data_perturb, prior)
    out = out.reshape(2, models, blocks, layers, LANES).transpose(0, 1, 3, 2, 4)
    return out.reshape(2, models, layers, layer_cells)


def solution(mesh):
    return jax.shard_map(
        body,
        mesh=mesh,
        in_specs=(
            P(None, ("slab", "dp"), "cell"),
            P(None, ("slab", "dp")),
            P(None, ("slab", "dp")),
            P(None, ("slab", "dp")),
            P(None, None, ("slab", "dp")),
            P(None, "slab", "cell", None),
        ),
        out_specs=P(None, "slab", "cell", None),
        check_vma=False,
    )
```

```python
import functools

import jax
import jax.numpy as jnp
from jax import lax
from jax.experimental import pallas as pl
from jax.experimental.pallas import tpu as pltpu
from jax.sharding import PartitionSpec as P

NX = 32
NZ = 32
NSURV = 8
ITERS = 4
LANES = 128
MODELS = 8
PARTS = 1
SLOTS = 3

nu_value = 4.0
step_size = 0.5
couple_weight = 0.02
prior_weight = 0.1

MESH = pl.DeviceIdType.MESH


def split_rows(value):
    high = value.astype(jnp.bfloat16).astype(jnp.float32)
    return jnp.concatenate([high, value - high], axis=0).astype(jnp.bfloat16)


def fold_rows(value):
    half = value.shape[0] // 2
    return value[:half] + value[half:]


def cross_gradients(first, second, masks, layer_cells, z_on):
    along_x, along_y = masks

    def differences(field, deeper):
        diff_x = (pltpu.roll(field, layer_cells - 1, 1) - field) * along_x
        diff_y = (pltpu.roll(field, layer_cells - NX, 1) - field) * along_y
        return diff_x, diff_y, (deeper - field) * z_on

    a = differences(*first)
    b = differences(*second)
    tx = a[1] * b[2] - a[2] * b[1]
    ty = a[2] * b[0] - a[0] * b[2]
    tz = a[0] * b[1] - a[1] * b[0]
    scaling = 2.0 / (1.0 + tx * tx + ty * ty + tz * tz)
    sx = scaling * along_x
    sy = scaling * along_y
    sz = scaling * z_on
    return (
        (sx * (b[1] * tz - b[2] * ty), sy * (b[2] * tx - b[0] * tz), sz * (b[0] * ty - b[1] * tx)),
        (sx * (ty * a[2] - tz * a[1]), sy * (tz * a[0] - tx * a[2]), sz * (tx * a[1] - ty * a[0])),
    )


def kernel(
    cells, layers, sens, observed_in, noise_in, ids_in, perturb_in, prior_in, result_out,
    observed, noise, survey_ids, perturb, prior_raw, prior, out, result, raw, high, low, high_t, low_t, base, carry_z, halo_up, halo_dn, acc, gather, target, per_noise, resids,
    count_tile, sums_mine, sums_other, rows, grad_mine, grad_other,
    input_sem, result_sem, load_sem, halo_send, halo_recv, part_send, part_recv, sums_send, sums_recv, grad_send, grad_recv,
):
    stations = observed.shape[1]
    layer_cells = prior.shape[3]
    blocks = layer_cells // LANES
    tiles = stations // LANES
    slab = lax.axis_index("slab")
    me = lax.axis_index("cell")
    dp = lax.axis_index("dp")
    partner = 1 - dp
    width = layer_cells // PARTS
    order = sorted(range(layers), key=lambda l: 0 < l < layers - 1)
    pieces = [(l, slice(h * width, (h + 1) * width)) for l in order for h in range(PARTS)]

    def load(n):
        s, l = n // layers, lax.rem(n, layers)
        slot = lax.rem(n, SLOTS)
        return pltpu.make_async_copy(
            sens.at[s, :, pl.ds(pl.multiple_of(l * layer_cells, LANES), layer_cells)], raw.at[slot],
            load_sem.at[slot],
        )

    inputs = [
        pltpu.make_async_copy(source, kept, input_sem.at[i])
        for i, (source, kept) in enumerate((
            (prior_in, prior_raw), (observed_in, observed), (noise_in, noise), (ids_in, survey_ids),
            (perturb_in, perturb),
        ))
    ]
    for copy in inputs:
        copy.start()
    for n in range(SLOTS - 1):
        load(jnp.int32(n)).start()

    barrier = pltpu.get_barrier_semaphore()
    pl.semaphore_signal(barrier, inc=1, device_id=(slab, me, partner), device_id_type=MESH)
    for k in range(1, cells):
        there = lax.rem(me + k, cells)
        pl.semaphore_signal(barrier, inc=1, device_id=(slab, there, dp), device_id_type=MESH)

    position = lax.broadcasted_iota(jnp.int32, (1, layer_cells), 1)
    masks = (
        (lax.rem(position, NX) < NX - 1).astype(jnp.float32),
        (position < layer_cells - NX).astype(jnp.float32),
    )
    lane = lax.broadcasted_iota(jnp.int32, (8, LANES), 1)

    @pl.when(me == cells - 1)
    def _():
        halo_up[...] = jnp.zeros_like(halo_up)

    @pl.when(me == 0)
    def _():
        halo_dn[...] = jnp.zeros_like(halo_dn)

    def rows_of(l, j):
        return pl.ds(j * layers + l, MODELS, stride=blocks * layers)

    for copy in inputs:
        copy.wait()
    for s in range(2):
        for l in range(layers):
            for j in range(blocks):
                prior[s, l, :, j * LANES : (j + 1) * LANES] = prior_raw[s, rows_of(l, j), :]

    def ids_at(s, t):
        return jnp.broadcast_to(survey_ids[s : s + 1, t * LANES : (t + 1) * LANES], (8, LANES))

    def by_survey(s, values, offset):
        total = jnp.zeros((8, LANES), jnp.float32)
        ids = [ids_at(s, t) for t in range(tiles)]
        for j in range(NSURV):
            one = jnp.where(ids[0] == j, values[0], 0.0)
            for t in range(1, tiles):
                one = one + jnp.where(ids[t] == j, values[t], 0.0)
            total = jnp.where(lane == j + offset, jnp.sum(one, axis=1, keepdims=True), total)
        return total

    for s in range(2):
        count_tile[s] = by_survey(s, [jnp.ones((8, LANES), jnp.float32)] * tiles, NSURV)
        scale = noise[s : s + 1]
        target[s] = observed[s : s + 1] + scale * perturb[s]
        per_noise[s] = jnp.broadcast_to(1.0 / scale, per_noise.shape[1:])

    def halo_copy(source, it, s, up):
        return pltpu.make_async_remote_copy(
            src_ref=source.at[s, 0 if up else layers - 1],
            dst_ref=(halo_up if up else halo_dn).at[it, s],
            send_sem=halo_send.at[s, 0 if up else 1],
            recv_sem=halo_recv.at[it, s, 0 if up else 1],
            device_id=(slab, jnp.maximum(me - 1, 0) if up else jnp.minimum(me + 1, cells - 1), dp),
            device_id_type=MESH,
        )

    def start_halo(source, it, s, l):
        if l == 0:
            @pl.when(me > 0)
            def _():
                halo_copy(source, it, s, True).start()

        if l == layers - 1:
            @pl.when(me < cells - 1)
            def _():
                halo_copy(source, it, s, False).start()

    def wait_halo_sent(source, it, s):
        @pl.when(me > 0)
        def _():
            halo_copy(source, it, s, True).wait_send()

        @pl.when(me < cells - 1)
        def _():
            halo_copy(source, it, s, False).wait_send()

    def wait_halos_here(source, it):
        @pl.when(me < cells - 1)
        def _():
            for s in range(2):
                halo_copy(source, it, s, True).wait_recv()

        @pl.when(me > 0)
        def _():
            for s in range(2):
                halo_copy(source, it, s, False).wait_recv()

    def send_parts(it, s, total):
        gather[it, s, me] = fold_rows(total)
        for k in range(1, cells):
            pltpu.make_async_remote_copy(
                src_ref=gather.at[it, s, me], dst_ref=gather.at[it, s, me],
                send_sem=part_send.at[s], recv_sem=part_recv.at[it, s],
                device_id=(slab, lax.rem(me + k, cells), dp), device_id_type=MESH,
            ).start()

    def wait_parts_sent(it, s):
        sent = gather.at[it, s, pl.ds(0, cells - 1)]
        pltpu.make_async_copy(sent, sent, part_send.at[s]).wait()

    def sums_copy(it, s):
        return pltpu.make_async_remote_copy(
            src_ref=sums_mine.at[it, s], dst_ref=sums_other.at[it, s],
            send_sem=sums_send.at[s], recv_sem=sums_recv.at[it, s],
            device_id=(slab, me, partner), device_id_type=MESH,
        )

    def residuals(it, s):
        got = gather.at[it, s, pl.ds(0, cells - 1)]
        pltpu.make_async_copy(got, got, part_recv.at[it, s]).wait()
        squares = []
        for t in range(tiles):
            span = slice(t * LANES, (t + 1) * LANES)
            predicted = gather[it, s, 0, :, span]
            for c in range(1, cells):
                predicted = predicted + gather[it, s, c, :, span]
            resid = (predicted - target[s, :, span]) * per_noise[s, :, span]
            resids[s, :, span] = resid
            squares.append(resid * resid)
        sums_mine[it, s] = by_survey(s, squares, 0) + count_tile[s]
        sums_copy(it, s).start()

    def weigh(it, s):
        sums_copy(it, s).wait_recv()
        sums = sums_mine[it, s] + sums_other[it, s]
        counts = pltpu.roll(sums, LANES - NSURV, 1)
        per_root = lax.rsqrt((sums + 1.0) / (counts + 1.0))
        columns = [jnp.broadcast_to(per_root[:, j : j + 1], (8, LANES)) for j in range(NSURV)]
        for t in range(tiles):
            span = slice(t * LANES, (t + 1) * LANES)
            ids = ids_at(s, t)
            per_scale = columns[0]
            for j in range(1, NSURV):
                per_scale = jnp.where(ids == j, columns[j], per_scale)
            whitened = resids[s, :, span] * per_scale
            factor = (
                (nu_value + 1.0) * whitened * (per_noise[s, :, span] * per_scale)
                / (nu_value + whitened * whitened)
            )
            rows[s, :, span] = split_rows(factor)

    def grad_copy(it, s, p):
        return pltpu.make_async_remote_copy(
            src_ref=grad_mine.at[s, p], dst_ref=grad_other.at[it, s, p],
            send_sem=grad_send.at[s, p], recv_sem=grad_recv.at[it, s, p],
            device_id=(slab, me, partner), device_id_type=MESH,
        )

    def gradient(it, s, beside):
        factor = rows[s]

        def finish(p, product):
            grad_mine[s, p] = fold_rows(product)
            grad_copy(it, s, p).start()

        held = None
        for p, (l, span) in enumerate(pieces):
            product = jnp.dot(factor, high[s, l, :, span], preferred_element_type=jnp.float32)
            product = product + jnp.dot(factor, low[s, l, :, span], preferred_element_type=jnp.float32)
            beside(p)
            if held is not None:
                finish(p - 1, held)
            held = product
        finish(len(pieces) - 1, held)

    def predict(s, l, span, value):
        model = split_rows(value)
        product = jnp.dot(model, high_t[s, l, span], preferred_element_type=jnp.float32)
        return product + jnp.dot(model, low_t[s, l, span], preferred_element_type=jnp.float32)

    def couple(source, it, l):
        if l == layers - 1:
            wait_halos_here(source, it)
        z_on = (me * layers + l < NZ - 1).astype(jnp.float32)
        first, second = [
            (source[s, l], source[s, l + 1] if l < layers - 1 else halo_up[it, s]) for s in range(2)
        ]
        both = cross_gradients(first, second, masks, layer_cells, z_on)
        for s in range(2):
            gx, gy, gz = both[s]
            total = pltpu.roll(gx, 1, 1) - gx + (pltpu.roll(gy, NX, 1) - gy) - gz
            if l > 0:
                total = total + carry_z[s]
            carry_z[s] = gz
            field = source[s, l]
            base[s, l] = field - step_size * (
                couple_weight * total + prior_weight * (field - prior[s, l])
            )

    def couple_below(source, it):
        z_on = (me > 0).astype(jnp.float32)
        first, second = [(halo_dn[it, s], source[s, 0]) for s in range(2)]
        both = cross_gradients(first, second, masks, layer_cells, z_on)
        for s in range(2):
            base[s, 0] -= step_size * couple_weight * both[s][2]

    def advance(source, it, s, last):
        wait_halo_sent(source, it, s)
        total = jnp.zeros((2 * MODELS, stations), jnp.float32)
        for p, (l, span) in enumerate(pieces):
            grad_copy(it, s, p).wait_recv()
            value = base[s, l, :, span] - step_size * (grad_mine[s, p] + grad_other[it, s, p])
            if last:
                for j in range(width // LANES):
                    result[s, rows_of(l, span.start // LANES + j), :] = value[:, j * LANES : (j + 1) * LANES]
            else:
                out[s, l, :, span] = value
                if p % PARTS == PARTS - 1:
                    start_halo(out, it + 1, s, l)
                total = total + predict(s, l, span, value)
        wait_parts_sent(it, s)
        if not last:
            send_parts(it + 1, s, total)
        if last:
            pltpu.make_async_copy(result.at[s], result_out.at[s], result_sem.at[s]).start()
        sums_copy(it, s).wait_send()
        for p in range(len(pieces)):
            grad_copy(it, s, p).wait_send()

    def step(source, it, last):
        residuals(it, 0)
        for l in range(layers - 1):
            couple(source, it, l)
        weigh(it, 0)

        def beside(p):
            if p == max(len(pieces) - 4, 0):
                couple(source, it, layers - 1)
            if p == len(pieces) - 2:
                couple_below(source, it)

        gradient(it, 0, beside)
        advance(source, it, 0, last)
        residuals(it, 1)
        weigh(it, 1)
        gradient(it, 1, lambda p: None)
        advance(source, it, 1, last)

    pl.semaphore_wait(barrier, cells)
    for s in range(2):
        for l in range(layers):
            start_halo(prior, 0, s, l)
    for s in range(2):
        acc[...] = jnp.zeros_like(acc)

        @pl.loop(0, layers)
        def _(l, s=s):
            n = s * layers + l
            load(n).wait()

            @pl.when(n + SLOTS - 1 < 2 * layers)
            def _():
                load(n + SLOTS - 1).start()

            value = raw[lax.rem(n, SLOTS)]
            rounded = value.astype(jnp.bfloat16)
            high[s, l] = rounded
            low[s, l] = (value - rounded.astype(jnp.float32)).astype(jnp.bfloat16)
            high_t[s, l] = high[s, l].T
            low_t[s, l] = low[s, l].T
            acc[...] += predict(s, l, slice(0, layer_cells), prior[s, l])

        send_parts(0, s, acc[...])

    step(prior, 0, ITERS == 1)
    if ITERS > 2:
        @pl.loop(1, ITERS - 1)
        def _(it):
            step(out, it, False)
    if ITERS > 1:
        step(out, ITERS - 1, True)
    for s in range(2):
        pltpu.make_async_copy(result.at[s], result_out.at[s], result_sem.at[s]).wait()


def body(sens, observed, noise, survey_ids, data_perturb, prior):
    cells = lax.axis_size("cell")
    models, layers, layer_cells = prior.shape[1:]
    stations = observed.shape[1]
    tiles = stations // LANES
    pieces, width = layers * PARTS, layer_cells // PARTS
    assert models == MODELS and stations % LANES == 0 and width % LANES == 0
    assert lax.axis_size("dp") == 2
    f32, bf16 = jnp.float32, jnp.bfloat16
    field = (2, layers, models, layer_cells)
    blocks = layer_cells // LANES
    flat = (2, models * blocks * layers, LANES)
    vmem = pl.BlockSpec(memory_space=pltpu.VMEM)
    dma = pltpu.SemaphoreType.DMA
    prior = prior.reshape(2, models, layers, blocks, LANES).transpose(0, 1, 3, 2, 4).reshape(flat)
    out = pl.pallas_call(
        functools.partial(kernel, cells, layers),
        out_shape=jax.ShapeDtypeStruct(flat, f32),
        in_specs=[pl.BlockSpec(memory_space=pltpu.HBM)] * 6,
        out_specs=pl.BlockSpec(memory_space=pl.ANY),
        scratch_shapes=[
            pltpu.VMEM((2, stations), f32),
            pltpu.VMEM((2, stations), f32),
            pltpu.VMEM((2, stations), jnp.int32),
            pltpu.VMEM((2, models, stations), f32),
            pltpu.VMEM(flat, f32),
            pltpu.VMEM(field, f32),
            pltpu.VMEM(field, f32),
            pltpu.VMEM(flat, f32),
            pltpu.VMEM((SLOTS, stations, layer_cells), f32),
            pltpu.VMEM((2, layers, stations, layer_cells), bf16),
            pltpu.VMEM((2, layers, stations, layer_cells), bf16),
            pltpu.VMEM((2, layers, layer_cells, stations), bf16),
            pltpu.VMEM((2, layers, layer_cells, stations), bf16),
            pltpu.VMEM(field, f32),
            pltpu.VMEM((2, models, layer_cells), f32),
            pltpu.VMEM((ITERS, 2, models, layer_cells), f32),
            pltpu.VMEM((ITERS, 2, models, layer_cells), f32),
            pltpu.VMEM((2 * models, stations), f32),
            pltpu.VMEM((ITERS, 2, cells, models, stations), f32),
            pltpu.VMEM((2, models, stations), f32),
            pltpu.VMEM((2, models, stations), f32),
            pltpu.VMEM((2, models, stations), f32),
            pltpu.VMEM((2, models, LANES), f32),
            pltpu.VMEM((ITERS, 2, models, LANES), f32),
            pltpu.VMEM((ITERS, 2, models, LANES), f32),
            pltpu.VMEM((2, 2 * models, stations), bf16),
            pltpu.VMEM((2, pieces, models, width), f32),
            pltpu.VMEM((ITERS, 2, pieces, models, width), f32),
            dma((5,)),
            dma((2,)),
            dma((SLOTS,)),
            dma((2, 2)),
            dma((ITERS, 2, 2)),
            dma((2,)),
            dma((ITERS, 2)),
            dma((2,)),
            dma((ITERS, 2)),
            dma((2, pieces)),
            dma((ITERS, 2, pieces)),
        ],
        compiler_params=pltpu.CompilerParams(
            collective_id=0, has_side_effects=True, vmem_limit_bytes=52000 * 1024
        ),
    )(*[pltpu.with_memory_space_constraint(x, pltpu.HBM) for x in (sens, observed, noise, survey_ids, data_perturb, prior)])
    out = out.reshape(2, models, blocks, layers, LANES).transpose(0, 1, 3, 2, 4)
    return out.reshape(2, models, layers, layer_cells)


def solution(mesh):
    return jax.shard_map(
        body,
        mesh=mesh,
        in_specs=(
            P(None, ("slab", "dp"), "cell"),
            P(None, ("slab", "dp")),
            P(None, ("slab", "dp")),
            P(None, ("slab", "dp")),
            P(None, None, ("slab", "dp")),
            P(None, "slab", "cell", None),
        ),
        out_specs=P(None, "slab", "cell", None),
        check_vma=False,
    )
```

```python
import functools

import jax
import jax.numpy as jnp
from jax import lax
from jax.experimental import pallas as pl
from jax.experimental.pallas import tpu as pltpu
from jax.sharding import PartitionSpec as P

NX = 32
NZ = 32
NSURV = 8
ITERS = 4
LANES = 128
MODELS = 8
PARTS = 1
SLOTS = 3

nu_value = 4.0
step_size = 0.5
couple_weight = 0.02
prior_weight = 0.1

MESH = pl.DeviceIdType.MESH


def split_rows(value):
    high = value.astype(jnp.bfloat16).astype(jnp.float32)
    return jnp.concatenate([high, value - high], axis=0).astype(jnp.bfloat16)


def fold_rows(value):
    half = value.shape[0] // 2
    return value[:half] + value[half:]


def cross_gradients(first, second, masks, layer_cells, z_on):
    along_x, along_y = masks

    def differences(field, deeper):
        diff_x = (pltpu.roll(field, layer_cells - 1, 1) - field) * along_x
        diff_y = (pltpu.roll(field, layer_cells - NX, 1) - field) * along_y
        return diff_x, diff_y, (deeper - field) * z_on

    a = differences(*first)
    b = differences(*second)
    tx = a[1] * b[2] - a[2] * b[1]
    ty = a[2] * b[0] - a[0] * b[2]
    tz = a[0] * b[1] - a[1] * b[0]
    scaling = 2.0 / (1.0 + tx * tx + ty * ty + tz * tz)
    sx = scaling * along_x
    sy = scaling * along_y
    sz = scaling * z_on
    return (
        (sx * (b[1] * tz - b[2] * ty), sy * (b[2] * tx - b[0] * tz), sz * (b[0] * ty - b[1] * tx)),
        (sx * (ty * a[2] - tz * a[1]), sy * (tz * a[0] - tx * a[2]), sz * (tx * a[1] - ty * a[0])),
    )


def kernel(
    cells, layers, sens, observed_in, noise_in, ids_in, perturb_in, prior_in, result,
    observed, noise, survey_ids, perturb, prior_raw, prior, out, raw, high, low, high_t, low_t, base, carry_z, halo_up, halo_dn, acc, gather, target, per_noise, resids,
    count_tile, sums_mine, sums_other, rows, grad_mine, grad_other,
    input_sem, load_sem, halo_send, halo_recv, part_send, part_recv, sums_send, sums_recv, grad_send, grad_recv,
):
    stations = observed.shape[1]
    layer_cells = prior.shape[3]
    blocks = layer_cells // LANES
    tiles = stations // LANES
    slab = lax.axis_index("slab")
    me = lax.axis_index("cell")
    dp = lax.axis_index("dp")
    partner = 1 - dp
    width = layer_cells // PARTS
    order = sorted(range(layers), key=lambda l: 0 < l < layers - 1)
    pieces = [(l, slice(h * width, (h + 1) * width)) for l in order for h in range(PARTS)]

    def load(n):
        s, l = n // layers, lax.rem(n, layers)
        slot = lax.rem(n, SLOTS)
        return pltpu.make_async_copy(
            sens.at[s, :, pl.ds(pl.multiple_of(l * layer_cells, LANES), layer_cells)], raw.at[slot],
            load_sem.at[slot],
        )

    inputs = [
        pltpu.make_async_copy(source, kept, input_sem.at[i])
        for i, (source, kept) in enumerate((
            (prior_in, prior_raw), (observed_in, observed), (noise_in, noise), (ids_in, survey_ids),
            (perturb_in, perturb),
        ))
    ]
    for copy in inputs:
        copy.start()
    for n in range(SLOTS - 1):
        load(jnp.int32(n)).start()

    barrier = pltpu.get_barrier_semaphore()
    pl.semaphore_signal(barrier, inc=1, device_id=(slab, me, partner), device_id_type=MESH)
    for k in range(1, cells):
        there = lax.rem(me + k, cells)
        pl.semaphore_signal(barrier, inc=1, device_id=(slab, there, dp), device_id_type=MESH)

    position = lax.broadcasted_iota(jnp.int32, (1, layer_cells), 1)
    masks = (
        (lax.rem(position, NX) < NX - 1).astype(jnp.float32),
        (position < layer_cells - NX).astype(jnp.float32),
    )
    lane = lax.broadcasted_iota(jnp.int32, (8, LANES), 1)

    @pl.when(me == cells - 1)
    def _():
        halo_up[...] = jnp.zeros_like(halo_up)

    @pl.when(me == 0)
    def _():
        halo_dn[...] = jnp.zeros_like(halo_dn)

    def rows_of(l, j):
        return pl.ds(j * layers + l, MODELS, stride=blocks * layers)

    for copy in inputs:
        copy.wait()
    for s in range(2):
        for l in range(layers):
            for j in range(blocks):
                prior[s, l, :, j * LANES : (j + 1) * LANES] = prior_raw[s, rows_of(l, j), :]

    def ids_at(s, t):
        return jnp.broadcast_to(survey_ids[s : s + 1, t * LANES : (t + 1) * LANES], (8, LANES))

    def by_survey(s, values, offset):
        total = jnp.zeros((8, LANES), jnp.float32)
        ids = [ids_at(s, t) for t in range(tiles)]
        for j in range(NSURV):
            one = jnp.where(ids[0] == j, values[0], 0.0)
            for t in range(1, tiles):
                one = one + jnp.where(ids[t] == j, values[t], 0.0)
            total = jnp.where(lane == j + offset, jnp.sum(one, axis=1, keepdims=True), total)
        return total

    for s in range(2):
        count_tile[s] = by_survey(s, [jnp.ones((8, LANES), jnp.float32)] * tiles, NSURV)
        scale = noise[s : s + 1]
        target[s] = observed[s : s + 1] + scale * perturb[s]
        per_noise[s] = jnp.broadcast_to(1.0 / scale, per_noise.shape[1:])

    def halo_copy(source, it, s, up):
        return pltpu.make_async_remote_copy(
            src_ref=source.at[s, 0 if up else layers - 1],
            dst_ref=(halo_up if up else halo_dn).at[it, s],
            send_sem=halo_send.at[s, 0 if up else 1],
            recv_sem=halo_recv.at[it, s, 0 if up else 1],
            device_id=(slab, jnp.maximum(me - 1, 0) if up else jnp.minimum(me + 1, cells - 1), dp),
            device_id_type=MESH,
        )

    def start_halo(source, it, s, l):
        if l == 0:
            @pl.when(me > 0)
            def _():
                halo_copy(source, it, s, True).start()

        if l == layers - 1:
            @pl.when(me < cells - 1)
            def _():
                halo_copy(source, it, s, False).start()

    def wait_halo_sent(source, it, s):
        @pl.when(me > 0)
        def _():
            halo_copy(source, it, s, True).wait_send()

        @pl.when(me < cells - 1)
        def _():
            halo_copy(source, it, s, False).wait_send()

    def wait_halos_here(source, it):
        @pl.when(me < cells - 1)
        def _():
            for s in range(2):
                halo_copy(source, it, s, True).wait_recv()

        @pl.when(me > 0)
        def _():
            for s in range(2):
                halo_copy(source, it, s, False).wait_recv()

    def send_parts(it, s, total):
        gather[it, s, me] = fold_rows(total)
        for k in range(1, cells):
            pltpu.make_async_remote_copy(
                src_ref=gather.at[it, s, me], dst_ref=gather.at[it, s, me],
                send_sem=part_send.at[s], recv_sem=part_recv.at[it, s],
                device_id=(slab, lax.rem(me + k, cells), dp), device_id_type=MESH,
            ).start()

    def wait_parts_sent(it, s):
        sent = gather.at[it, s, pl.ds(0, cells - 1)]
        pltpu.make_async_copy(sent, sent, part_send.at[s]).wait()

    def sums_copy(it, s):
        return pltpu.make_async_remote_copy(
            src_ref=sums_mine.at[it, s], dst_ref=sums_other.at[it, s],
            send_sem=sums_send.at[s], recv_sem=sums_recv.at[it, s],
            device_id=(slab, me, partner), device_id_type=MESH,
        )

    def residuals(it, s):
        got = gather.at[it, s, pl.ds(0, cells - 1)]
        pltpu.make_async_copy(got, got, part_recv.at[it, s]).wait()
        squares = []
        for t in range(tiles):
            span = slice(t * LANES, (t + 1) * LANES)
            predicted = gather[it, s, 0, :, span]
            for c in range(1, cells):
                predicted = predicted + gather[it, s, c, :, span]
            resid = (predicted - target[s, :, span]) * per_noise[s, :, span]
            resids[s, :, span] = resid
            squares.append(resid * resid)
        sums_mine[it, s] = by_survey(s, squares, 0) + count_tile[s]
        sums_copy(it, s).start()

    def weigh(it, s):
        sums_copy(it, s).wait_recv()
        sums = sums_mine[it, s] + sums_other[it, s]
        counts = pltpu.roll(sums, LANES - NSURV, 1)
        per_root = lax.rsqrt((sums + 1.0) / (counts + 1.0))
        columns = [jnp.broadcast_to(per_root[:, j : j + 1], (8, LANES)) for j in range(NSURV)]
        for t in range(tiles):
            span = slice(t * LANES, (t + 1) * LANES)
            ids = ids_at(s, t)
            per_scale = columns[0]
            for j in range(1, NSURV):
                per_scale = jnp.where(ids == j, columns[j], per_scale)
            whitened = resids[s, :, span] * per_scale
            factor = (
                (nu_value + 1.0) * whitened * (per_noise[s, :, span] * per_scale)
                / (nu_value + whitened * whitened)
            )
            rows[s, :, span] = split_rows(factor)

    def grad_copy(it, s, p):
        return pltpu.make_async_remote_copy(
            src_ref=grad_mine.at[s, p], dst_ref=grad_other.at[it, s, p],
            send_sem=grad_send.at[s, p], recv_sem=grad_recv.at[it, s, p],
            device_id=(slab, me, partner), device_id_type=MESH,
        )

    def gradient(it, s, beside):
        factor = rows[s]

        def finish(p, product):
            grad_mine[s, p] = fold_rows(product)
            grad_copy(it, s, p).start()

        held = None
        for p, (l, span) in enumerate(pieces):
            product = jnp.dot(factor, high[s, l, :, span], preferred_element_type=jnp.float32)
            product = product + jnp.dot(factor, low[s, l, :, span], preferred_element_type=jnp.float32)
            beside(p)
            if held is not None:
                finish(p - 1, held)
            held = product
        finish(len(pieces) - 1, held)

    def predict(s, l, span, value):
        model = split_rows(value)
        product = jnp.dot(model, high_t[s, l, span], preferred_element_type=jnp.float32)
        return product + jnp.dot(model, low_t[s, l, span], preferred_element_type=jnp.float32)

    def couple(source, it, l):
        if l == layers - 1:
            wait_halos_here(source, it)
        z_on = (me * layers + l < NZ - 1).astype(jnp.float32)
        first, second = [
            (source[s, l], source[s, l + 1] if l < layers - 1 else halo_up[it, s]) for s in range(2)
        ]
        both = cross_gradients(first, second, masks, layer_cells, z_on)
        for s in range(2):
            gx, gy, gz = both[s]
            total = pltpu.roll(gx, 1, 1) - gx + (pltpu.roll(gy, NX, 1) - gy) - gz
            if l > 0:
                total = total + carry_z[s]
            carry_z[s] = gz
            field = source[s, l]
            base[s, l] = field - step_size * (
                couple_weight * total + prior_weight * (field - prior[s, l])
            )

    def couple_below(source, it):
        z_on = (me > 0).astype(jnp.float32)
        first, second = [(halo_dn[it, s], source[s, 0]) for s in range(2)]
        both = cross_gradients(first, second, masks, layer_cells, z_on)
        for s in range(2):
            base[s, 0] -= step_size * couple_weight * both[s][2]

    def advance(source, it, s, last):
        wait_halo_sent(source, it, s)
        total = jnp.zeros((2 * MODELS, stations), jnp.float32)
        for p, (l, span) in enumerate(pieces):
            grad_copy(it, s, p).wait_recv()
            value = base[s, l, :, span] - step_size * (grad_mine[s, p] + grad_other[it, s, p])
            if last:
                for j in range(width // LANES):
                    result[s, rows_of(l, span.start // LANES + j), :] = value[:, j * LANES : (j + 1) * LANES]
            else:
                out[s, l, :, span] = value
                if p % PARTS == PARTS - 1:
                    start_halo(out, it + 1, s, l)
                total = total + predict(s, l, span, value)
        wait_parts_sent(it, s)
        if not last:
            send_parts(it + 1, s, total)
        sums_copy(it, s).wait_send()
        for p in range(len(pieces)):
            grad_copy(it, s, p).wait_send()

    def step(source, it, last):
        residuals(it, 0)
        for l in range(layers - 1):
            couple(source, it, l)
        weigh(it, 0)

        def beside(p):
            if p == max(len(pieces) - 4, 0):
                couple(source, it, layers - 1)
            if p == len(pieces) - 2:
                couple_below(source, it)

        gradient(it, 0, beside)
        advance(source, it, 0, last)
        residuals(it, 1)
        weigh(it, 1)
        gradient(it, 1, lambda p: None)
        advance(source, it, 1, last)

    pl.semaphore_wait(barrier, cells)
    for s in range(2):
        for l in range(layers):
            start_halo(prior, 0, s, l)
    for s in range(2):
        acc[...] = jnp.zeros_like(acc)

        @pl.loop(0, layers)
        def _(l, s=s):
            n = s * layers + l
            load(n).wait()

            @pl.when(n + SLOTS - 1 < 2 * layers)
            def _():
                load(n + SLOTS - 1).start()

            value = raw[lax.rem(n, SLOTS)]
            rounded = value.astype(jnp.bfloat16)
            high[s, l] = rounded
            low[s, l] = (value - rounded.astype(jnp.float32)).astype(jnp.bfloat16)
            high_t[s, l] = high[s, l].T
            low_t[s, l] = low[s, l].T
            acc[...] += predict(s, l, slice(0, layer_cells), prior[s, l])

        send_parts(0, s, acc[...])

    step(prior, 0, ITERS == 1)
    if ITERS > 2:
        @pl.loop(1, ITERS - 1)
        def _(it):
            step(out, it, False)
    if ITERS > 1:
        step(out, ITERS - 1, True)


def body(sens, observed, noise, survey_ids, data_perturb, prior):
    cells = lax.axis_size("cell")
    models, layers, layer_cells = prior.shape[1:]
    stations = observed.shape[1]
    tiles = stations // LANES
    pieces, width = layers * PARTS, layer_cells // PARTS
    assert models == MODELS and stations % LANES == 0 and width % LANES == 0
    assert lax.axis_size("dp") == 2
    f32, bf16 = jnp.float32, jnp.bfloat16
    field = (2, layers, models, layer_cells)
    blocks = layer_cells // LANES
    flat = (2, models * blocks * layers, LANES)
    vmem = pl.BlockSpec(memory_space=pltpu.VMEM)
    dma = pltpu.SemaphoreType.DMA
    prior = prior.reshape(2, models, layers, blocks, LANES).transpose(0, 1, 3, 2, 4).reshape(flat)
    out = pl.pallas_call(
        functools.partial(kernel, cells, layers),
        out_shape=jax.ShapeDtypeStruct(flat, f32),
        in_specs=[pl.BlockSpec(memory_space=pltpu.HBM)] * 6,
        out_specs=vmem,
        scratch_shapes=[
            pltpu.VMEM((2, stations), f32),
            pltpu.VMEM((2, stations), f32),
            pltpu.VMEM((2, stations), jnp.int32),
            pltpu.VMEM((2, models, stations), f32),
            pltpu.VMEM(flat, f32),
            pltpu.VMEM(field, f32),
            pltpu.VMEM(field, f32),
            pltpu.VMEM((SLOTS, stations, layer_cells), f32),
            pltpu.VMEM((2, layers, stations, layer_cells), bf16),
            pltpu.VMEM((2, layers, stations, layer_cells), bf16),
            pltpu.VMEM((2, layers, layer_cells, stations), bf16),
            pltpu.VMEM((2, layers, layer_cells, stations), bf16),
            pltpu.VMEM(field, f32),
            pltpu.VMEM((2, models, layer_cells), f32),
            pltpu.VMEM((ITERS, 2, models, layer_cells), f32),
            pltpu.VMEM((ITERS, 2, models, layer_cells), f32),
            pltpu.VMEM((2 * models, stations), f32),
            pltpu.VMEM((ITERS, 2, cells, models, stations), f32),
            pltpu.VMEM((2, models, stations), f32),
            pltpu.VMEM((2, models, stations), f32),
            pltpu.VMEM((2, models, stations), f32),
            pltpu.VMEM((2, models, LANES), f32),
            pltpu.VMEM((ITERS, 2, models, LANES), f32),
            pltpu.VMEM((ITERS, 2, models, LANES), f32),
            pltpu.VMEM((2, 2 * models, stations), bf16),
            pltpu.VMEM((2, pieces, models, width), f32),
            pltpu.VMEM((ITERS, 2, pieces, models, width), f32),
            dma((5,)),
            dma((SLOTS,)),
            dma((2, 2)),
            dma((ITERS, 2, 2)),
            dma((2,)),
            dma((ITERS, 2)),
            dma((2,)),
            dma((ITERS, 2)),
            dma((2, pieces)),
            dma((ITERS, 2, pieces)),
        ],
        compiler_params=pltpu.CompilerParams(
            collective_id=0, has_side_effects=True, vmem_limit_bytes=52000 * 1024
        ),
    )(*[pltpu.with_memory_space_constraint(x, pltpu.HBM) for x in (sens, observed, noise, survey_ids, data_perturb, prior)])
    out = out.reshape(2, models, blocks, layers, LANES).transpose(0, 1, 3, 2, 4)
    return out.reshape(2, models, layers, layer_cells)


def solution(mesh):
    return jax.shard_map(
        body,
        mesh=mesh,
        in_specs=(
            P(None, ("slab", "dp"), "cell"),
            P(None, ("slab", "dp")),
            P(None, ("slab", "dp")),
            P(None, ("slab", "dp")),
            P(None, None, ("slab", "dp")),
            P(None, "slab", "cell", None),
        ),
        out_specs=P(None, "slab", "cell", None),
        check_vma=False,
    )
```

```python
import functools

import jax
import jax.numpy as jnp
from jax import lax
from jax.experimental import pallas as pl
from jax.experimental.pallas import tpu as pltpu
from jax.sharding import PartitionSpec as P

NX = 32
NZ = 32
NSURV = 8
ITERS = 4
LANES = 128
MODELS = 8
PARTS = 1
SLOTS = 3

nu_value = 4.0
step_size = 0.5
couple_weight = 0.02
prior_weight = 0.1

MESH = pl.DeviceIdType.MESH


def split_rows(value):
    high = value.astype(jnp.bfloat16).astype(jnp.float32)
    return jnp.concatenate([high, value - high], axis=0).astype(jnp.bfloat16)


def fold_rows(value):
    half = value.shape[0] // 2
    return value[:half] + value[half:]


def cross_gradients(first, second, masks, layer_cells, z_on):
    along_x, along_y = masks

    def differences(field, deeper):
        diff_x = (pltpu.roll(field, layer_cells - 1, 1) - field) * along_x
        diff_y = (pltpu.roll(field, layer_cells - NX, 1) - field) * along_y
        return diff_x, diff_y, (deeper - field) * z_on

    a = differences(*first)
    b = differences(*second)
    tx = a[1] * b[2] - a[2] * b[1]
    ty = a[2] * b[0] - a[0] * b[2]
    tz = a[0] * b[1] - a[1] * b[0]
    scaling = 2.0 / (1.0 + tx * tx + ty * ty + tz * tz)
    sx = scaling * along_x
    sy = scaling * along_y
    sz = scaling * z_on
    return (
        (sx * (b[1] * tz - b[2] * ty), sy * (b[2] * tx - b[0] * tz), sz * (b[0] * ty - b[1] * tx)),
        (sx * (ty * a[2] - tz * a[1]), sy * (tz * a[0] - tx * a[2]), sz * (tx * a[1] - ty * a[0])),
    )


def kernel(
    cells, layers, sens, observed_in, noise_in, ids_in, perturb_in, prior_in, result,
    observed, noise, survey_ids, perturb, prior_raw, prior, out, raw, high, low, high_t, low_t, base, carry_z, halo_up, halo_dn, acc, gather, target, per_noise, resids,
    count_tile, sums_mine, sums_other, rows, grad_mine, grad_other,
    input_sem, load_sem, halo_send, halo_recv, part_send, part_recv, sums_send, sums_recv, grad_send, grad_recv,
):
    stations = observed.shape[1]
    layer_cells = prior.shape[3]
    blocks = layer_cells // LANES
    tiles = stations // LANES
    slab = lax.axis_index("slab")
    me = lax.axis_index("cell")
    dp = lax.axis_index("dp")
    partner = 1 - dp
    width = layer_cells // PARTS
    order = sorted(range(layers), key=lambda l: 0 < l < layers - 1)
    pieces = [(l, slice(h * width, (h + 1) * width)) for l in order for h in range(PARTS)]

    def load(n):
        s, l = n // layers, lax.rem(n, layers)
        slot = lax.rem(n, SLOTS)
        return pltpu.make_async_copy(
            sens.at[s, :, pl.ds(pl.multiple_of(l * layer_cells, LANES), layer_cells)], raw.at[slot],
            load_sem.at[slot],
        )

    inputs = [
        pltpu.make_async_copy(source, kept, input_sem.at[i])
        for i, (source, kept) in enumerate((
            (prior_in, prior_raw), (observed_in, observed), (noise_in, noise), (ids_in, survey_ids),
            (perturb_in, perturb),
        ))
    ]
    for copy in inputs:
        copy.start()
    for n in range(SLOTS - 1):
        load(jnp.int32(n)).start()

    barrier = pltpu.get_barrier_semaphore()
    pl.semaphore_signal(barrier, inc=1, device_id=(slab, me, partner), device_id_type=MESH)
    for k in range(1, cells):
        there = lax.rem(me + k, cells)
        pl.semaphore_signal(barrier, inc=1, device_id=(slab, there, dp), device_id_type=MESH)

    position = lax.broadcasted_iota(jnp.int32, (1, layer_cells), 1)
    masks = (
        (lax.rem(position, NX) < NX - 1).astype(jnp.float32),
        (position < layer_cells - NX).astype(jnp.float32),
    )
    lane = lax.broadcasted_iota(jnp.int32, (8, LANES), 1)

    @pl.when(me == cells - 1)
    def _():
        halo_up[...] = jnp.zeros_like(halo_up)

    @pl.when(me == 0)
    def _():
        halo_dn[...] = jnp.zeros_like(halo_dn)

    def rows_of(l, j):
        return pl.ds(j * layers + l, MODELS, stride=blocks * layers)

    for copy in inputs:
        copy.wait()
    for s in range(2):
        for l in range(layers):
            for j in range(blocks):
                prior[s, l, :, j * LANES : (j + 1) * LANES] = prior_raw[s, rows_of(l, j), :]

    def ids_at(s, t):
        return jnp.broadcast_to(survey_ids[s : s + 1, t * LANES : (t + 1) * LANES], (8, LANES))

    def by_survey(s, values, offset):
        total = jnp.zeros((8, LANES), jnp.float32)
        ids = [ids_at(s, t) for t in range(tiles)]
        for j in range(NSURV):
            one = jnp.where(ids[0] == j, values[0], 0.0)
            for t in range(1, tiles):
                one = one + jnp.where(ids[t] == j, values[t], 0.0)
            total = jnp.where(lane == j + offset, jnp.sum(one, axis=1, keepdims=True), total)
        return total

    for s in range(2):
        count_tile[s] = by_survey(s, [jnp.ones((8, LANES), jnp.float32)] * tiles, NSURV)
        scale = noise[s : s + 1]
        target[s] = observed[s : s + 1] + scale * perturb[s]
        per_noise[s] = jnp.broadcast_to(1.0 / scale, per_noise.shape[1:])

    def halo_copy(source, it, s, up):
        return pltpu.make_async_remote_copy(
            src_ref=source.at[s, 0 if up else layers - 1],
            dst_ref=(halo_up if up else halo_dn).at[it, s],
            send_sem=halo_send.at[s, 0 if up else 1],
            recv_sem=halo_recv.at[it, s, 0 if up else 1],
            device_id=(slab, jnp.maximum(me - 1, 0) if up else jnp.minimum(me + 1, cells - 1), dp),
            device_id_type=MESH,
        )

    def start_halo(source, it, s, l):
        if l == 0:
            @pl.when(me > 0)
            def _():
                halo_copy(source, it, s, True).start()

        if l == layers - 1:
            @pl.when(me < cells - 1)
            def _():
                halo_copy(source, it, s, False).start()

    def wait_halo_sent(source, it, s):
        @pl.when(me > 0)
        def _():
            halo_copy(source, it, s, True).wait_send()

        @pl.when(me < cells - 1)
        def _():
            halo_copy(source, it, s, False).wait_send()

    def wait_halos_here(source, it):
        @pl.when(me < cells - 1)
        def _():
            for s in range(2):
                halo_copy(source, it, s, True).wait_recv()

        @pl.when(me > 0)
        def _():
            for s in range(2):
                halo_copy(source, it, s, False).wait_recv()

    def send_parts(it, s, total):
        gather[it, s, me] = fold_rows(total)
        for k in range(1, cells):
            pltpu.make_async_remote_copy(
                src_ref=gather.at[it, s, me], dst_ref=gather.at[it, s, me],
                send_sem=part_send.at[s], recv_sem=part_recv.at[it, s],
                device_id=(slab, lax.rem(me + k, cells), dp), device_id_type=MESH,
            ).start()

    def wait_parts_sent(it, s):
        sent = gather.at[it, s, pl.ds(0, cells - 1)]
        pltpu.make_async_copy(sent, sent, part_send.at[s]).wait()

    def sums_copy(it, s):
        return pltpu.make_async_remote_copy(
            src_ref=sums_mine.at[it, s], dst_ref=sums_other.at[it, s],
            send_sem=sums_send.at[s], recv_sem=sums_recv.at[it, s],
            device_id=(slab, me, partner), device_id_type=MESH,
        )

    def residuals(it, s):
        got = gather.at[it, s, pl.ds(0, cells - 1)]
        pltpu.make_async_copy(got, got, part_recv.at[it, s]).wait()
        squares = []
        for t in range(tiles):
            span = slice(t * LANES, (t + 1) * LANES)
            predicted = gather[it, s, 0, :, span]
            for c in range(1, cells):
                predicted = predicted + gather[it, s, c, :, span]
            resid = (predicted - target[s, :, span]) * per_noise[s, :, span]
            resids[s, :, span] = resid
            squares.append(resid * resid)
        sums_mine[it, s] = by_survey(s, squares, 0) + count_tile[s]
        sums_copy(it, s).start()

    def weigh(it, s):
        sums_copy(it, s).wait_recv()
        sums = sums_mine[it, s] + sums_other[it, s]
        counts = pltpu.roll(sums, LANES - NSURV, 1)
        per_root = lax.rsqrt((sums + 1.0) / (counts + 1.0))
        columns = [jnp.broadcast_to(per_root[:, j : j + 1], (8, LANES)) for j in range(NSURV)]
        for t in range(tiles):
            span = slice(t * LANES, (t + 1) * LANES)
            ids = ids_at(s, t)
            per_scale = columns[0]
            for j in range(1, NSURV):
                per_scale = jnp.where(ids == j, columns[j], per_scale)
            whitened = resids[s, :, span] * per_scale
            factor = (
                (nu_value + 1.0) * whitened * (per_noise[s, :, span] * per_scale)
                / (nu_value + whitened * whitened)
            )
            rows[s, :, span] = split_rows(factor)

    def grad_copy(it, s, p):
        return pltpu.make_async_remote_copy(
            src_ref=grad_mine.at[s, p], dst_ref=grad_other.at[it, s, p],
            send_sem=grad_send.at[s, p], recv_sem=grad_recv.at[it, s, p],
            device_id=(slab, me, partner), device_id_type=MESH,
        )

    def gradient(it, s, beside):
        factor = rows[s]

        def finish(p, product):
            grad_mine[s, p] = fold_rows(product)
            grad_copy(it, s, p).start()

        held = None
        for p, (l, span) in enumerate(pieces):
            product = jnp.dot(factor, high[s, l, :, span], preferred_element_type=jnp.float32)
            product = product + jnp.dot(factor, low[s, l, :, span], preferred_element_type=jnp.float32)
            beside(p)
            if held is not None:
                finish(p - 1, held)
            held = product
        finish(len(pieces) - 1, held)

    def predict(s, l, span, value):
        model = split_rows(value)
        product = jnp.dot(model, high_t[s, l, span], preferred_element_type=jnp.float32)
        return product + jnp.dot(model, low_t[s, l, span], preferred_element_type=jnp.float32)

    def couple(source, it, l):
        if l == layers - 1:
            wait_halos_here(source, it)
        z_on = (me * layers + l < NZ - 1).astype(jnp.float32)
        first, second = [
            (source[s, l], source[s, l + 1] if l < layers - 1 else halo_up[it, s]) for s in range(2)
        ]
        both = cross_gradients(first, second, masks, layer_cells, z_on)
        for s in range(2):
            gx, gy, gz = both[s]
            total = pltpu.roll(gx, 1, 1) - gx + (pltpu.roll(gy, NX, 1) - gy) - gz
            if l > 0:
                total = total + carry_z[s]
            carry_z[s] = gz
            field = source[s, l]
            base[s, l] = field - step_size * (
                couple_weight * total + prior_weight * (field - prior[s, l])
            )

    def couple_below(source, it):
        z_on = (me > 0).astype(jnp.float32)
        first, second = [(halo_dn[it, s], source[s, 0]) for s in range(2)]
        both = cross_gradients(first, second, masks, layer_cells, z_on)
        for s in range(2):
            base[s, 0] -= step_size * couple_weight * both[s][2]

    def advance(source, it, s, last):
        wait_halo_sent(source, it, s)
        total = jnp.zeros((2 * MODELS, stations), jnp.float32)
        for p, (l, span) in enumerate(pieces):
            grad_copy(it, s, p).wait_recv()
            value = base[s, l, :, span] - step_size * (grad_mine[s, p] + grad_other[it, s, p])
            if last:
                for j in range(width // LANES):
                    result[s, rows_of(l, span.start // LANES + j), :] = value[:, j * LANES : (j + 1) * LANES]
            else:
                out[s, l, :, span] = value
                if p % PARTS == PARTS - 1:
                    start_halo(out, it + 1, s, l)
                total = total + predict(s, l, span, value)
        wait_parts_sent(it, s)
        if not last:
            send_parts(it + 1, s, total)
        sums_copy(it, s).wait_send()
        for p in range(len(pieces)):
            grad_copy(it, s, p).wait_send()

    def step(source, it, last):
        residuals(it, 0)
        for l in range(layers - 1):
            couple(source, it, l)
        weigh(it, 0)

        def beside(p):
            if p == max(len(pieces) - 4, 0):
                couple(source, it, layers - 1)
            if p == len(pieces) - 2:
                couple_below(source, it)

        gradient(it, 0, beside)
        if last:
            residuals(it, 1)
        advance(source, it, 0, last)
        if not last:
            residuals(it, 1)
        weigh(it, 1)
        gradient(it, 1, lambda p: None)
        advance(source, it, 1, last)

    pl.semaphore_wait(barrier, cells)
    for s in range(2):
        for l in range(layers):
            start_halo(prior, 0, s, l)
    for s in range(2):
        acc[...] = jnp.zeros_like(acc)

        @pl.loop(0, layers)
        def _(l, s=s):
            n = s * layers + l
            load(n).wait()

            @pl.when(n + SLOTS - 1 < 2 * layers)
            def _():
                load(n + SLOTS - 1).start()

            value = raw[lax.rem(n, SLOTS)]
            rounded = value.astype(jnp.bfloat16)
            high[s, l] = rounded
            low[s, l] = (value - rounded.astype(jnp.float32)).astype(jnp.bfloat16)
            high_t[s, l] = high[s, l].T
            low_t[s, l] = low[s, l].T
            acc[...] += predict(s, l, slice(0, layer_cells), prior[s, l])

        send_parts(0, s, acc[...])

    step(prior, 0, ITERS == 1)
    if ITERS > 2:
        @pl.loop(1, ITERS - 1)
        def _(it):
            step(out, it, False)
    if ITERS > 1:
        step(out, ITERS - 1, True)


def body(sens, observed, noise, survey_ids, data_perturb, prior):
    cells = lax.axis_size("cell")
    models, layers, layer_cells = prior.shape[1:]
    stations = observed.shape[1]
    tiles = stations // LANES
    pieces, width = layers * PARTS, layer_cells // PARTS
    assert models == MODELS and stations % LANES == 0 and width % LANES == 0
    assert lax.axis_size("dp") == 2
    f32, bf16 = jnp.float32, jnp.bfloat16
    field = (2, layers, models, layer_cells)
    blocks = layer_cells // LANES
    flat = (2, models * blocks * layers, LANES)
    vmem = pl.BlockSpec(memory_space=pltpu.VMEM)
    dma = pltpu.SemaphoreType.DMA
    prior = prior.reshape(2, models, layers, blocks, LANES).transpose(0, 1, 3, 2, 4).reshape(flat)
    out = pl.pallas_call(
        functools.partial(kernel, cells, layers),
        out_shape=jax.ShapeDtypeStruct(flat, f32),
        in_specs=[pl.BlockSpec(memory_space=pltpu.HBM)] * 6,
        out_specs=vmem,
        scratch_shapes=[
            pltpu.VMEM((2, stations), f32),
            pltpu.VMEM((2, stations), f32),
            pltpu.VMEM((2, stations), jnp.int32),
            pltpu.VMEM((2, models, stations), f32),
            pltpu.VMEM(flat, f32),
            pltpu.VMEM(field, f32),
            pltpu.VMEM(field, f32),
            pltpu.VMEM((SLOTS, stations, layer_cells), f32),
            pltpu.VMEM((2, layers, stations, layer_cells), bf16),
            pltpu.VMEM((2, layers, stations, layer_cells), bf16),
            pltpu.VMEM((2, layers, layer_cells, stations), bf16),
            pltpu.VMEM((2, layers, layer_cells, stations), bf16),
            pltpu.VMEM(field, f32),
            pltpu.VMEM((2, models, layer_cells), f32),
            pltpu.VMEM((ITERS, 2, models, layer_cells), f32),
            pltpu.VMEM((ITERS, 2, models, layer_cells), f32),
            pltpu.VMEM((2 * models, stations), f32),
            pltpu.VMEM((ITERS, 2, cells, models, stations), f32),
            pltpu.VMEM((2, models, stations), f32),
            pltpu.VMEM((2, models, stations), f32),
            pltpu.VMEM((2, models, stations), f32),
            pltpu.VMEM((2, models, LANES), f32),
            pltpu.VMEM((ITERS, 2, models, LANES), f32),
            pltpu.VMEM((ITERS, 2, models, LANES), f32),
            pltpu.VMEM((2, 2 * models, stations), bf16),
            pltpu.VMEM((2, pieces, models, width), f32),
            pltpu.VMEM((ITERS, 2, pieces, models, width), f32),
            dma((5,)),
            dma((SLOTS,)),
            dma((2, 2)),
            dma((ITERS, 2, 2)),
            dma((2,)),
            dma((ITERS, 2)),
            dma((2,)),
            dma((ITERS, 2)),
            dma((2, pieces)),
            dma((ITERS, 2, pieces)),
        ],
        compiler_params=pltpu.CompilerParams(
            collective_id=0, has_side_effects=True, vmem_limit_bytes=52000 * 1024
        ),
    )(*[pltpu.with_memory_space_constraint(x, pltpu.HBM) for x in (sens, observed, noise, survey_ids, data_perturb, prior)])
    out = out.reshape(2, models, blocks, layers, LANES).transpose(0, 1, 3, 2, 4)
    return out.reshape(2, models, layers, layer_cells)


def solution(mesh):
    return jax.shard_map(
        body,
        mesh=mesh,
        in_specs=(
            P(None, ("slab", "dp"), "cell"),
            P(None, ("slab", "dp")),
            P(None, ("slab", "dp")),
            P(None, ("slab", "dp")),
            P(None, None, ("slab", "dp")),
            P(None, "slab", "cell", None),
        ),
        out_specs=P(None, "slab", "cell", None),
        check_vma=False,
    )
```
